32 devices in a mesh: seq: 4 (over z), dp: 8 (over y, x, core).
Axes of the slice: x: 2, y: 2, z: 4, core: 2. Of those that a mesh axis runs over, the one named last changes fastest.
Arguments:
- tokens: bfloat16 [8, 512, 2048], P('dp', 'seq'), may hold values from -6 to 6
- doc_lengths: int32 [8, 12], P('dp'), may hold values from 1 to 256, 512 in all within a row
- qkv_weight: bfloat16 [2048, 6144], P(('seq', 'dp')), may hold values from -0.125 to 0.125
- qv_bias: bfloat16 [4096], P(('seq', 'dp')), may hold values from -3 to 3
- out_weight: bfloat16 [2048, 2048], P(('seq', 'dp')), may hold values from -1.5 to 1.5
- out_bias: bfloat16 [2048], P(('seq', 'dp')), may hold values from -3 to 3
- norm1_gain: bfloat16 [2048], P(('seq', 'dp')), may hold values from 0.5 to 1.5
- norm1_bias: bfloat16 [2048], P(('seq', 'dp')), may hold values from -3 to 3
- in_weight: bfloat16 [2048, 8192], P(('seq', 'dp')), may hold values from -0.125 to 0.125
- in_bias: bfloat16 [8192], P(('seq', 'dp')), may hold values from -3 to 3
- down_weight: bfloat16 [8192, 2048], P(('seq', 'dp')), may hold values from -0.0625 to 0.0625
- down_bias: bfloat16 [2048], P(('seq', 'dp')), may hold values from -3 to 3
- norm2_gain: bfloat16 [2048], P(('seq', 'dp')), may hold values from 0.5 to 1.5
- norm2_bias: bfloat16 [2048], P(('seq', 'dp')), may hold values from -3 to 3
- cotangent: bfloat16 [8, 512, 2048], P('dp', 'seq'), may hold values from -6 to 6
Outputs:
- output: bfloat16 [8, 512, 2048], P('dp', 'seq')
- input_grad: bfloat16 [8, 512, 2048], P('dp', 'seq')
- qkv_weight_grad: float32 [2048, 6144], P(('seq', 'dp'))
- qv_bias_grad: float32 [4096], P(('seq', 'dp'))
- out_weight_grad: float32 [2048, 2048], P(('seq', 'dp'))
- out_bias_grad: float32 [2048], P(('seq', 'dp'))
- norm1_gain_grad: float32 [2048], P(('seq', 'dp'))
- norm1_bias_grad: float32 [2048], P(('seq', 'dp'))
- in_weight_grad: float32 [2048, 8192], P(('seq', 'dp'))
- in_bias_grad: float32 [8192], P(('seq', 'dp'))
- down_weight_grad: float32 [8192, 2048], P(('seq', 'dp'))
- down_bias_grad: float32 [2048], P(('seq', 'dp'))
- norm2_gain_grad: float32 [2048], P(('seq', 'dp'))
- norm2_bias_grad: float32 [2048], P(('seq', 'dp'))
The draws below stay inside these ranges and needn't reach their ends.
Inputs may be any that keep to these rules, and one draw needn't show every extreme that they name: `doc_lengths`: each row sums to 512, and its largest entry is exactly 256.
All inputs are finite; a program needn't handle non-finite values.
Results may differ from the reference program's by a relative error of at most 0.015.
Values may be sent and summed in bfloat16 or wider, within the bound.
No kernel may reach another device: no remote copies, remote signals or barrier semaphores. Data moves between devices by JAX's collectives and lax.ppermute only.
A program may use at most 384 MiB of HBM per device.

```python
import math
import jax
import jax.numpy as jnp
import numpy as np
from jax import lax

D = 2048
HEADS = 16
HEAD_DIM = 128
FF = 8192
DOCS = 12
SEQ_LEN = 512
SEQS = 8
DOC_MOST = 256


def block_levels(stream_key, dims, split, least, largest):
    level, own = 1.0, jax.random.fold_in(stream_key, 6)
    for position, parts in split:
        steps = jnp.exp(jax.random.uniform(jax.random.fold_in(own, position), (parts,), jnp.float32, least / len(split), largest / len(split)))
        level = level * jnp.repeat(steps, dims[position] // parts).reshape([-1 if axis == position else 1 for axis in range(len(dims))])
    return level


def profile(amount, total, bound, skew):
    portions = [(1 << 20) // math.isqrt(grade ** skew) + 1 for grade in range(2, amount + 1)]
    spare, counts = total - bound - (amount - 1), [1] * (amount - 1)
    while spare > 0:
        candidates = [i for i in range(amount - 1) if counts[i] < bound]
        whole, budget = sum([portions[i] for i in candidates]), spare
        for i in candidates:
            addition = min(bound - counts[i], max(1, budget * portions[i] // whole), spare)
            counts[i] = counts[i] + addition
            spare = spare - addition
    return np.array([bound] + counts)


def ragged(own_key, count, total, bound, skew):
    if count == 2:
        one = jax.random.randint(own_key, (), max(1, total - bound), min(bound, total - 1) + 1)
        return jnp.stack([one, total - one])
    sizes = jnp.asarray(profile(count, total, bound, skew), jnp.int32)
    pairs = (count - 1) // 2
    giver, receiver = sizes[1:1 + 2 * pairs:2], sizes[2:2 + 2 * pairs:2]
    room = jnp.minimum(giver - 1, bound - receiver)
    passed = jax.random.randint(jax.random.fold_in(own_key, 1), (pairs,), 0, 1 << 20) % (room + 1)
    sizes = sizes.at[1:1 + 2 * pairs:2].set(giver - passed).at[2:2 + 2 * pairs:2].set(receiver + passed)
    return sizes[jax.random.permutation(jax.random.fold_in(own_key, 2), count)]


def scatter_about(own_key, extent, deviation, bound, split=(), held_as=jnp.bfloat16):
    array = jax.random.normal(own_key, extent, jnp.float32) * deviation
    if len(split) > 0:
        array = block_levels(own_key, extent, split, -0.22, 0.18) * array
    return jnp.clip(array, min=-bound, max=bound).astype(held_as)


def setup_inputs(seed: int = 0) -> dict:
    keys = jax.random.split(jax.random.key(seed), 16)
    return {
        "tokens": scatter_about(keys[0], (SEQS, SEQ_LEN, D), 1.0, 6.0, ((0, 8), (1, 4))),
        "doc_lengths": jax.vmap(lambda own: ragged(own, DOCS, SEQ_LEN, DOC_MOST, 2))(jax.random.split(keys[1], SEQS)).reshape((SEQS, DOCS)).astype(jnp.int32),
        "qkv_weight": scatter_about(keys[2], (D, 3 * D), D ** -0.5, 0.125, ((0, 32),)),
        "qv_bias": scatter_about(keys[3], (2 * D,), 0.5, 3.0, ((0, 32),)),
        "out_weight": scatter_about(keys[4], (D, D), (D // 128) ** -0.5, 1.5, ((0, 32),)),
        "out_bias": scatter_about(keys[5], (D,), 0.5, 3.0, ((0, 32),)),
        "norm1_gain": jnp.clip(1.0 + 0.1 * jax.random.normal(keys[6], (D,), jnp.float32), 0.5, 1.5).astype(jnp.bfloat16),
        "norm1_bias": scatter_about(keys[7], (D,), 0.5, 3.0, ((0, 32),)),
        "in_weight": scatter_about(keys[8], (D, FF), D ** -0.5, 0.125, ((0, 32),)),
        "in_bias": scatter_about(keys[9], (FF,), 0.5, 3.0, ((0, 32),)),
        "down_weight": scatter_about(keys[10], (FF, D), FF ** -0.5, 0.0625, ((0, 32),)),
        "down_bias": scatter_about(keys[11], (D,), 0.5, 3.0, ((0, 32),)),
        "norm2_gain": jnp.clip(1.0 + 0.1 * jax.random.normal(keys[12], (D,), jnp.float32), 0.5, 1.5).astype(jnp.bfloat16),
        "norm2_bias": scatter_about(keys[13], (D,), 0.5, 3.0, ((0, 32),)),
        "cotangent": scatter_about(keys[14], (SEQS, SEQ_LEN, D), 1.0, 6.0, ((0, 8), (1, 4))),
    }


@jax.custom_vjp
def low(v):
    return lax.optimization_barrier(v.astype(jnp.bfloat16)).astype(jnp.float32)

@jax.custom_vjp
def low_back(v):
    return v

def low_keep(v):
    return (low(v), None)

def low_pass(kept, grad):
    return (grad,)

def back_keep(v):
    return (v, None)

def back_low(kept, grad):
    return (low(grad),)
low.defvjp(low_keep, low_pass)
low_back.defvjp(back_keep, back_low)
highest = lax.Precision.HIGHEST
eps_norm = 1e-06

def segment_ids(lengths, total):
    ends = jnp.cumsum(lengths.astype(jnp.int32))
    places = jnp.arange(total, dtype=jnp.int32)
    return lax.optimization_barrier(jnp.sum((places[:, None] >= ends[None, :]).astype(jnp.int32), axis=1)).astype(jnp.int32)

def layer_norm(hidden, gain, shift):
    center = hidden - lax.optimization_barrier(jnp.mean(hidden, axis=-1, keepdims=True))
    spread = lax.optimization_barrier(jnp.mean(center * center, axis=-1, keepdims=True))
    return center * lax.rsqrt(spread + eps_norm) * gain + shift

def forward(tok_rows, params, segment):
    qkv_w, qv_b, out_w, out_b, gain_one, shift_one, in_w, in_b, down_w, down_b, gain_two, shift_two = params
    seq_length = tok_rows.shape[0]
    zero_bias = jnp.zeros((D,), jnp.float32)
    full_bias = jnp.concatenate([qv_b[:D], zero_bias, qv_b[D:]])
    qkv = low(low_back(jnp.dot(tok_rows, qkv_w, precision=highest) + full_bias))
    queries = qkv[:, :D].reshape(seq_length, HEADS, HEAD_DIM)
    keys_all = qkv[:, D:2 * D].reshape(seq_length, HEADS, HEAD_DIM)
    values_all = qkv[:, 2 * D:].reshape(seq_length, HEADS, HEAD_DIM)
    block_rows = min(512, seq_length)

    def attend(pieces):
        query_block, seg_block = pieces
        scores = jnp.einsum('thd,khd->htk', query_block, keys_all, precision=highest) * HEAD_DIM ** (-0.5)
        scores = low_back(scores)
        matches = (seg_block[:, None] == segment[None, :])[None]
        probs = jax.nn.softmax(jnp.where(matches, scores, -1e+30), axis=-1)
        probs = low(probs)
        return jnp.einsum('htk,khd->thd', probs, values_all, precision=highest)
    mixed = lax.map(jax.checkpoint(attend), (queries.reshape(seq_length // block_rows, block_rows, HEADS, HEAD_DIM), segment.reshape(seq_length // block_rows, block_rows)))
    mixed = low(low_back(mixed.reshape(seq_length, D)))
    attn = low_back(jnp.dot(mixed, out_w, precision=highest) + out_b)
    first = layer_norm(tok_rows + attn, gain_one, shift_one)
    first_low = low(first)
    pre = low_back(jnp.dot(first_low, in_w, precision=highest) + in_b)
    act = low(jax.nn.gelu(pre, approximate=True))
    ffn = low_back(jnp.dot(act, down_w, precision=highest) + down_b)
    return layer_norm(first + ffn, gain_two, shift_two)

def reference(tokens, doc_lengths, qkv_weight, qv_bias, out_weight, out_bias, norm1_gain, norm1_bias, in_weight, in_bias, down_weight, down_bias, norm2_gain, norm2_bias, cotangent):
    params = tuple((item.astype(jnp.float32) for item in (qkv_weight, qv_bias, out_weight, out_bias, norm1_gain, norm1_bias, in_weight, in_bias, down_weight, down_bias, norm2_gain, norm2_bias)))

    def sequence_step(totals, pieces):
        seq_tokens, seq_lengths, seq_cot = pieces
        segment = segment_ids(seq_lengths, SEQ_LEN)
        result, pullback = jax.vjp(lambda tok_rows, weights: forward(tok_rows, weights, segment), seq_tokens.astype(jnp.float32), params)
        grad_tokens, grad_params = pullback(seq_cot.astype(jnp.float32))
        totals = tuple((acc_total + grad_item for acc_total, grad_item in zip(totals, grad_params)))
        return (totals, (result.astype(jnp.bfloat16), grad_tokens.astype(jnp.bfloat16)))
    initial = tuple((jnp.zeros_like(item) for item in params))
    sums, (results, grads) = lax.scan(sequence_step, initial, (tokens, doc_lengths, cotangent))
    return (results, grads, sums[0], sums[1], sums[2], sums[3], sums[4], sums[5], sums[6], sums[7], sums[8], sums[9], sums[10], sums[11])
```

```python
import functools

import jax
import jax.numpy as jnp
from jax import lax
from jax.experimental import pallas as pl
from jax.experimental.pallas import tpu as pltpu
from jax.sharding import PartitionSpec as P

HEAD_DIM = 128
eps_norm = 1e-06
f32 = jnp.float32
bf16 = jnp.bfloat16
ALL = ("seq", "dp")


def shift(value, step):
    n = lax.axis_size("seq")
    return lax.ppermute(value, "seq", [(i, (i + step) % n) for i in range(n)])


def gather_seq(rows):
    n = lax.axis_size("seq")
    return jnp.concatenate([rows] + [shift(rows, k) for k in range(1, n)], axis=0)


def scatter_seq(partial):
    n = lax.axis_size("seq")
    count = partial.shape[0] // n
    total = partial[:count]
    for k in range(1, n):
        block = partial[k * count : (k + 1) * count].astype(bf16)
        total = total + shift(block, -k).astype(f32)
    return total


def normalize(hidden):
    center = hidden - jnp.mean(hidden, axis=-1, keepdims=True)
    spread = jnp.mean(center * center, axis=-1, keepdims=True)
    recip = lax.rsqrt(spread + eps_norm)
    return (center * recip, recip)


def norm_back(grad_out, normed, recip, gain):
    scaled = grad_out * gain
    return recip * (
        scaled
        - jnp.mean(scaled, axis=-1, keepdims=True)
        - normed * jnp.mean(scaled * normed, axis=-1, keepdims=True)
    )


def dot_nn(a, b):
    return lax.dot_general(a, b, (((1,), (0,)), ((), ())), preferred_element_type=f32)


def dot_nt(a, b):
    return lax.dot_general(a, b, (((1,), (1,)), ((), ())), preferred_element_type=f32)


def dot_tn(a, b):
    return lax.dot_general(a, b, (((0,), (0,)), ((), ())), preferred_element_type=f32)


def softmax_of(q, k, seg_col, seg_row):
    scores = dot_nt(q, k) * HEAD_DIM ** (-0.5)
    scores = jnp.where(seg_col == seg_row, scores, -1e30)
    terms = jnp.exp(scores - jnp.max(scores, axis=1, keepdims=True))
    return terms / jnp.sum(terms, axis=1, keepdims=True)


def attend_kernel(seg_col, seg_row, q, k, v, mixed):
    probs = softmax_of(q[...], k[...], seg_col[...], seg_row[...])
    mixed[...] = dot_nn(probs.astype(bf16), v[...]).astype(bf16)


def attend_back_kernel(seg_col, seg_row, q, k, v, gm, grad):
    heads = pl.num_programs(0)
    head = pl.program_id(0)
    probs = softmax_of(q[...], k[...], seg_col[...], seg_row[...])
    grad_probs = dot_nt(gm[...], v[...])
    products = jnp.sum(probs * grad_probs, axis=1, keepdims=True)
    grad_scores = (probs * (grad_probs - products)).astype(bf16)
    scale = HEAD_DIM ** (-0.5)

    def put(part, value):
        start = pl.multiple_of((part * heads + head) * HEAD_DIM, HEAD_DIM)
        grad[:, pl.ds(start, HEAD_DIM)] = value.astype(bf16)

    put(0, dot_nn(grad_scores, k[...]) * scale)
    put(1, dot_tn(grad_scores, q[...]) * scale)
    put(2, dot_tn(probs.astype(bf16), gm[...]))


def head_spec(rows, offset):
    return pl.BlockSpec((rows, HEAD_DIM), lambda h: (0, offset + h))


def attend(qkv, seg):
    rows, width = qkv.shape
    heads = width // (3 * HEAD_DIM)
    return pl.pallas_call(
        attend_kernel,
        grid=(heads,),
        in_specs=[
            pl.BlockSpec((rows, 1), lambda h: (0, 0)),
            pl.BlockSpec((1, rows), lambda h: (0, 0)),
            head_spec(rows, 0),
            head_spec(rows, heads),
            head_spec(rows, 2 * heads),
        ],
        out_specs=head_spec(rows, 0),
        out_shape=jax.ShapeDtypeStruct((rows, width // 3), bf16),
        compiler_params=pltpu.CompilerParams(vmem_limit_bytes=48 << 20),
        name="attend",
    )(seg[:, None], seg[None, :], qkv, qkv, qkv)


def attend_back(qkv, grad_mixed, seg):
    rows, width = qkv.shape
    heads = width // (3 * HEAD_DIM)
    return pl.pallas_call(
        attend_back_kernel,
        grid=(heads,),
        in_specs=[
            pl.BlockSpec((rows, 1), lambda h: (0, 0)),
            pl.BlockSpec((1, rows), lambda h: (0, 0)),
            head_spec(rows, 0),
            head_spec(rows, heads),
            head_spec(rows, 2 * heads),
            head_spec(rows, 0),
        ],
        out_specs=pl.BlockSpec((rows, width), lambda h: (0, 0)),
        out_shape=jax.ShapeDtypeStruct((rows, width), bf16),
        compiler_params=pltpu.CompilerParams(vmem_limit_bytes=48 << 20),
        name="attend_back",
    )(seg[:, None], seg[None, :], qkv, qkv, qkv, grad_mixed)


def columns_to_owner(shard, parts):
    n = lax.axis_size("seq")
    rows, width = shard.shape
    pieces = shard.reshape(rows, parts, n, width // (parts * n))
    pieces = pieces.transpose(2, 0, 1, 3).reshape(n, rows, width // n)
    moved = lax.all_to_all(pieces, "seq", 0, 0)
    full = lax.all_gather(moved, "dp", axis=1, tiled=True)
    return full.reshape(-1, width // n)


def columns_back(grad, parts):
    n = lax.axis_size("seq")
    width = grad.shape[1]
    stacked = grad.astype(bf16).reshape(n, -1, width)
    mine = lax.psum_scatter(stacked, "dp", scatter_dimension=1, tiled=True)
    moved = lax.all_to_all(mine, "seq", 0, 0)
    rows = moved.shape[1]
    moved = moved.reshape(n, rows, parts, width // parts).transpose(1, 2, 0, 3)
    return moved.reshape(rows, n * width).astype(f32)


def rows_back(grad):
    return lax.psum_scatter(grad.astype(bf16), "dp", scatter_dimension=0, tiled=True).astype(f32)


def all_small(vectors):
    count = lax.axis_size("seq") * lax.axis_size("dp")
    packed = jnp.concatenate(vectors)
    table = lax.all_to_all(jnp.broadcast_to(packed[None], (count, packed.shape[0])), ALL, 0, 0)
    out = []
    start = 0
    for vector in vectors:
        size = vector.shape[0]
        out.append(table[:, start : start + size].reshape(-1).astype(f32))
        start += size
    return out


def scatter_small(vectors):
    count = lax.axis_size("seq") * lax.axis_size("dp")
    packed = jnp.concatenate([v.reshape(count, -1) for v in vectors], axis=1)
    mine = jnp.sum(lax.all_to_all(packed, ALL, 0, 0), axis=0)
    out = []
    start = 0
    for vector in vectors:
        size = vector.shape[0] // count
        out.append(mine[start : start + size])
        start += size
    return out


def gelu_parts(v):
    c = 0.7978845608028654
    t = jnp.tanh(c * (v + 0.044715 * v * v * v))
    value = 0.5 * v * (1.0 + t)
    slope = 0.5 * (1.0 + t) + 0.5 * v * (1.0 - t * t) * c * (1.0 + 3 * 0.044715 * v * v)
    return value, slope


def per_device(
    tokens,
    doc_lengths,
    qkv_weight,
    qv_bias,
    out_weight,
    out_bias,
    norm1_gain,
    norm1_bias,
    in_weight,
    in_bias,
    down_weight,
    down_bias,
    norm2_gain,
    norm2_bias,
    cotangent,
):
    n = lax.axis_size("seq")
    s = lax.axis_index("seq")
    rows = tokens.shape[1]
    width = tokens.shape[2]
    part = width // n
    tok_rows = tokens[0]
    ends = jnp.cumsum(doc_lengths[0])
    steps = jnp.arange(n * rows, dtype=jnp.int32)
    places = jnp.remainder(s - steps // rows, n) * rows + steps % rows
    seg = jnp.sum((places[:, None] >= ends[None, :]).astype(jnp.int32), axis=1)

    small = all_small(
        [qv_bias, out_bias, norm1_gain, norm1_bias, in_bias, down_bias, norm2_gain, norm2_bias]
    )
    qv_full, out_b, gain_one, shift_one, in_b, down_b, gain_two, shift_two = small
    qkv_w = columns_to_owner(qkv_weight, 3)
    out_w = lax.all_gather(out_weight, "dp", axis=0, tiled=True)
    in_w = columns_to_owner(in_weight, 1)
    down_w = lax.all_gather(down_weight, "dp", axis=0, tiled=True)

    tok_full = gather_seq(tok_rows)
    q_bias = lax.dynamic_slice_in_dim(qv_full, s * part, part)
    v_bias = lax.dynamic_slice_in_dim(qv_full, width + s * part, part)
    qkv_b = jnp.concatenate([q_bias, jnp.zeros((part,), f32), v_bias])
    qkv = (dot_nn(tok_full, qkv_w) + qkv_b).astype(bf16)
    mixed = attend(qkv, seg)
    attn = scatter_seq(dot_nn(mixed, out_w)) + out_b
    normed_one, recip_one = normalize(tok_rows.astype(f32) + attn)
    first = normed_one * gain_one + shift_one
    first_full = gather_seq(first.astype(bf16))
    hidden = in_w.shape[1]
    pre = dot_nn(first_full, in_w) + lax.dynamic_slice_in_dim(in_b, s * hidden, hidden)
    act_value, act_slope = gelu_parts(pre)
    act = act_value.astype(bf16)
    ffn = scatter_seq(dot_nn(act, down_w)) + down_b
    normed_two, recip_two = normalize(first + ffn)
    result = (normed_two * gain_two + shift_two).astype(bf16)

    grad_out = cotangent[0].astype(f32)
    shift_two_grad = jnp.sum(grad_out, axis=0)
    gain_two_grad = jnp.sum(grad_out * normed_two, axis=0)
    grad_h2 = norm_back(grad_out, normed_two, recip_two, gain_two)
    grad_ffn = grad_h2.astype(bf16)
    down_b_grad = jnp.sum(grad_ffn.astype(f32), axis=0)
    grad_ffn_full = gather_seq(grad_ffn)
    grad_pre = (dot_nt(grad_ffn_full, down_w) * act_slope).astype(bf16)
    grad_first = grad_h2 + scatter_seq(dot_nt(grad_pre, in_w))
    down_w_grad = rows_back(dot_tn(act, grad_ffn_full))
    in_b_grad = jnp.sum(grad_pre.astype(f32), axis=0)
    in_w_grad = columns_back(dot_tn(first_full, grad_pre), 1)

    shift_one_grad = jnp.sum(grad_first, axis=0)
    gain_one_grad = jnp.sum(grad_first * normed_one, axis=0)
    grad_h1 = norm_back(grad_first, normed_one, recip_one, gain_one)
    grad_attn = grad_h1.astype(bf16)
    out_b_grad = jnp.sum(grad_attn.astype(f32), axis=0)
    grad_attn_full = gather_seq(grad_attn)
    grad_mixed = dot_nt(grad_attn_full, out_w).astype(bf16)
    grad_qkv = attend_back(qkv, grad_mixed, seg)
    out_w_grad = rows_back(dot_tn(mixed, grad_attn_full))
    qkv_w_grad = columns_back(dot_tn(tok_full, grad_qkv), 3)
    input_grad = (grad_h1 + scatter_seq(dot_nt(grad_qkv, qkv_w))).astype(bf16)

    sums = jnp.sum(grad_qkv.astype(f32), axis=0)
    qv_grad = jnp.zeros((2 * width,), f32)
    qv_grad = lax.dynamic_update_slice_in_dim(qv_grad, sums[:part], s * part, 0)
    qv_grad = lax.dynamic_update_slice_in_dim(qv_grad, sums[2 * part :], width + s * part, 0)
    in_b_all = jnp.zeros((n * hidden,), f32)
    in_b_all = lax.dynamic_update_slice_in_dim(in_b_all, in_b_grad, s * hidden, 0)
    small_grads = scatter_small(
        [
            qv_grad,
            out_b_grad,
            gain_one_grad,
            shift_one_grad,
            in_b_all,
            down_b_grad,
            gain_two_grad,
            shift_two_grad,
        ]
    )
    return (
        result[None],
        input_grad[None],
        qkv_w_grad,
        small_grads[0],
        out_w_grad,
        small_grads[1],
        small_grads[2],
        small_grads[3],
        in_w_grad,
        small_grads[4],
        down_w_grad,
        small_grads[5],
        small_grads[6],
        small_grads[7],
    )


def solution(mesh):
    rows = P(("seq", "dp"), None)
    flat = P(("seq", "dp"))
    tok = P("dp", "seq", None)
    return jax.shard_map(
        per_device,
        mesh=mesh,
        in_specs=(
            tok,
            P("dp", None),
            rows,
            flat,
            rows,
            flat,
            flat,
            flat,
            rows,
            flat,
            rows,
            flat,
            flat,
            flat,
            tok,
        ),
        out_specs=(tok, tok, rows, flat, rows, flat, flat, flat, rows, flat, rows, flat, flat, flat),
        check_vma=False,
    )
```

```python
import functools

import jax
import jax.numpy as jnp
from jax import lax
from jax.experimental import pallas as pl
from jax.experimental.pallas import tpu as pltpu
from jax.sharding import PartitionSpec as P

HEAD_DIM = 128
eps_norm = 1e-06
f32 = jnp.float32
bf16 = jnp.bfloat16
ALL = ("seq", "dp")


def shift(value, step):
    n = lax.axis_size("seq")
    return lax.ppermute(value, "seq", [(i, (i + step) % n) for i in range(n)])


def gather_blocks(rows):
    n = lax.axis_size("seq")
    return [rows] + [shift(rows, k) for k in range(1, n)]


def gather_seq(rows):
    return jnp.concatenate(gather_blocks(rows), axis=0)


def scatter_blocks(partial):
    n = lax.axis_size("seq")
    count = partial.shape[0] // n
    blocks = [partial[:count]]
    for k in range(1, n):
        blocks.append(shift(partial[k * count : (k + 1) * count].astype(bf16), -k))
    return blocks


def total_of(blocks):
    total = blocks[0]
    for block in blocks[1:]:
        total = total + block.astype(f32)
    return total


def scatter_seq(partial):
    return total_of(scatter_blocks(partial))


def normalize(hidden):
    center = hidden - jnp.mean(hidden, axis=-1, keepdims=True)
    spread = jnp.mean(center * center, axis=-1, keepdims=True)
    recip = lax.rsqrt(spread + eps_norm)
    return (center * recip, recip)


def norm_back(grad_out, normed, recip, gain):
    scaled = grad_out * gain
    return recip * (
        scaled
        - jnp.mean(scaled, axis=-1, keepdims=True)
        - normed * jnp.mean(scaled * normed, axis=-1, keepdims=True)
    )


def dot_nn(a, b):
    return lax.dot_general(a, b, (((1,), (0,)), ((), ())), preferred_element_type=f32)


def dot_nt(a, b):
    return lax.dot_general(a, b, (((1,), (1,)), ((), ())), preferred_element_type=f32)


def dot_tn(a, b):
    return lax.dot_general(a, b, (((0,), (0,)), ((), ())), preferred_element_type=f32)


def softmax_of(q, k, seg_col, seg_row):
    scores = dot_nt(q, k) * HEAD_DIM ** (-0.5)
    scores = jnp.where(seg_col == seg_row, scores, -1e30)
    terms = jnp.exp(scores - jnp.max(scores, axis=1, keepdims=True))
    return terms / jnp.sum(terms, axis=1, keepdims=True)


def attend_kernel(seg_col, seg_row, q, k, v, mixed):
    probs = softmax_of(q[...], k[...], seg_col[...], seg_row[...])
    mixed[...] = dot_nn(probs.astype(bf16), v[...]).astype(bf16)


def attend_back_kernel(seg_col, seg_row, q, k, v, gm, grad):
    heads = pl.num_programs(0)
    head = pl.program_id(0)
    probs = softmax_of(q[...], k[...], seg_col[...], seg_row[...])
    grad_probs = dot_nt(gm[...], v[...])
    products = jnp.sum(probs * grad_probs, axis=1, keepdims=True)
    grad_scores = (probs * (grad_probs - products)).astype(bf16)
    scale = HEAD_DIM ** (-0.5)

    def put(part, value):
        start = pl.multiple_of((part * heads + head) * HEAD_DIM, HEAD_DIM)
        grad[:, pl.ds(start, HEAD_DIM)] = value.astype(bf16)

    put(0, dot_nn(grad_scores, k[...]) * scale)
    put(1, dot_tn(grad_scores, q[...]) * scale)
    put(2, dot_tn(probs.astype(bf16), gm[...]))


def head_spec(rows, offset):
    return pl.BlockSpec((rows, HEAD_DIM), lambda h: (0, offset + h))


def attend(qkv, seg):
    rows, width = qkv.shape
    heads = width // (3 * HEAD_DIM)
    return pl.pallas_call(
        attend_kernel,
        grid=(heads,),
        in_specs=[
            pl.BlockSpec((rows, 1), lambda h: (0, 0)),
            pl.BlockSpec((1, rows), lambda h: (0, 0)),
            head_spec(rows, 0),
            head_spec(rows, heads),
            head_spec(rows, 2 * heads),
        ],
        out_specs=head_spec(rows, 0),
        out_shape=jax.ShapeDtypeStruct((rows, width // 3), bf16),
        compiler_params=pltpu.CompilerParams(vmem_limit_bytes=48 << 20),
        name="attend",
    )(seg[:, None], seg[None, :], qkv, qkv, qkv)


def attend_back(qkv, grad_mixed, seg):
    rows, width = qkv.shape
    heads = width // (3 * HEAD_DIM)
    return pl.pallas_call(
        attend_back_kernel,
        grid=(heads,),
        in_specs=[
            pl.BlockSpec((rows, 1), lambda h: (0, 0)),
            pl.BlockSpec((1, rows), lambda h: (0, 0)),
            head_spec(rows, 0),
            head_spec(rows, heads),
            head_spec(rows, 2 * heads),
            head_spec(rows, 0),
        ],
        out_specs=pl.BlockSpec((rows, width), lambda h: (0, 0)),
        out_shape=jax.ShapeDtypeStruct((rows, width), bf16),
        compiler_params=pltpu.CompilerParams(vmem_limit_bytes=48 << 20),
        name="attend_back",
    )(seg[:, None], seg[None, :], qkv, qkv, qkv, grad_mixed)


def after(value, *others):
    return lax.optimization_barrier((value, *others))[0]


def whole(kernel, out_shape, name, scalar, *args):
    spec = pltpu.PrefetchScalarGridSpec(
        num_scalar_prefetch=1,
        grid=(1,),
        in_specs=[pl.BlockSpec(arg.shape, lambda i, sc, r=arg.ndim: (0,) * r) for arg in args],
        out_specs=jax.tree.map(
            lambda o: pl.BlockSpec(o.shape, lambda i, sc, r=len(o.shape): (0,) * r), out_shape
        ),
    )
    params = pltpu.CompilerParams(vmem_limit_bytes=40 << 20)
    call = pl.pallas_call(
        kernel, grid_spec=spec, out_shape=out_shape, compiler_params=params, name=name
    )
    return call(jnp.reshape(scalar, (1,)).astype(jnp.int32), *args)


def pack_columns(shard, parts):
    n = lax.axis_size("seq")
    rows, width = shard.shape
    part = width // (parts * n)

    def kernel(s, shard_ref, *outs):
        for k in range(n):
            owner = jnp.remainder(s[0] + k, n)
            for p in range(parts):
                start = pl.multiple_of((p * n + owner) * part, part)
                outs[k][:, p * part : (p + 1) * part] = shard_ref[:, pl.ds(start, part)]

    out = [jax.ShapeDtypeStruct((rows, part * parts), shard.dtype)] * n
    return whole(kernel, out, "pack", lax.axis_index("seq"), shard)


def join_rows(blocks):
    n = len(blocks)
    shape = blocks[0].shape

    def kernel(s, *refs):
        for k in range(n):
            refs[n][jnp.remainder(s[0] - k + n, n)] = refs[k][...]

    out = jax.ShapeDtypeStruct((n, *shape), blocks[0].dtype)
    return whole(kernel, out, "join_rows", lax.axis_index("seq"), *blocks)


def join_columns(blocks, parts):
    n = len(blocks)
    rows, width = blocks[0].shape
    part = width // parts

    def kernel(s, *refs):
        for k in range(n):
            source = jnp.remainder(s[0] - k + n, n)
            for p in range(parts):
                start = pl.multiple_of((p * n + source) * part, part)
                piece = refs[k][:, p * part : (p + 1) * part]
                refs[n][:, pl.ds(start, part)] = piece.astype(f32)

    out = jax.ShapeDtypeStruct((rows, n * width), f32)
    return whole(kernel, out, "join_columns", lax.axis_index("seq"), *blocks)


def exchange(blocks):
    return [blocks[0]] + [shift(blocks[k], k) for k in range(1, len(blocks))]


def exchange_back(pieces):
    n = lax.axis_size("seq")
    s = lax.axis_index("seq")
    blocks = [
        lax.dynamic_index_in_dim(pieces, jnp.remainder(s + k, n), 0, keepdims=False)
        for k in range(n)
    ]
    return exchange(blocks)


def grid_call(kernel, grid, in_specs, out_specs, out_shape, name, args, **more):
    return pl.pallas_call(
        kernel,
        grid=grid,
        in_specs=in_specs,
        out_specs=out_specs,
        out_shape=out_shape,
        compiler_params=pltpu.CompilerParams(vmem_limit_bytes=48 << 20),
        name=name,
        **more,
    )(*args)


def feed_grads(n, groups, act, grad_ffn, first, grad_pre):
    tokens, hidden = act.shape
    width = grad_ffn.shape[1]
    down_rows = hidden // groups
    shard = down_rows // n
    shape = jax.ShapeDtypeStruct((2 * n, groups * shard, width), bf16)

    def down_kernel(a, b, out):
        out[...] = dot_tn(a[...], b[...]).astype(bf16).reshape(n, shard, width)

    part = grid_call(
        down_kernel,
        (groups,),
        [
            pl.BlockSpec((tokens, down_rows), lambda g: (0, g)),
            pl.BlockSpec((tokens, width), lambda g: (0, 0)),
        ],
        pl.BlockSpec((n, shard, width), lambda g: (0, g, 0)),
        shape,
        "down_grad",
        (act, grad_ffn),
    )
    rows = min(256, width // n)
    per = width // n // rows

    def in_kernel(a, b, before, out):
        out[0] = dot_tn(a[...], b[...]).astype(bf16)

    return grid_call(
        in_kernel,
        (width // rows,),
        [
            pl.BlockSpec((tokens, rows), lambda g: (0, g)),
            pl.BlockSpec((tokens, hidden), lambda g: (0, 0)),
            pl.BlockSpec(memory_space=pl.ANY),
        ],
        pl.BlockSpec((1, rows, hidden), lambda g: (n + g // per, g % per, 0)),
        shape,
        "in_grad",
        (first, grad_pre, part),
        input_output_aliases={2: 0},
    )


def attn_grads(n, tok, grad_qkv, mixed, grad_attn):
    tokens, width = tok.shape
    part = width // n
    rows = min(256, part)
    per = part // rows

    def kernel(x, g, m, ga, out):
        out[0, :, : 3 * part] = dot_tn(x[...], g[...]).astype(bf16)
        out[0, :, 3 * part :] = dot_tn(m[...], ga[...]).astype(bf16)

    return grid_call(
        kernel,
        (n, per),
        [
            pl.BlockSpec((tokens, rows), lambda j, h: (0, j * per + h)),
            pl.BlockSpec((tokens, 3 * part), lambda j, h: (0, 0)),
            pl.BlockSpec((tokens, rows), lambda j, h: (0, h)),
            pl.BlockSpec((tokens, part), lambda j, h: (0, j)),
        ],
        pl.BlockSpec((1, rows, 4 * part), lambda j, h: (j, h, 0)),
        jax.ShapeDtypeStruct((n, part, 4 * part), bf16),
        "attn_grads",
        (tok, grad_qkv, mixed, grad_attn),
    )


def gather_dp(shard):
    full = lax.all_gather(shard, "dp", axis=shard.ndim - 2, tiled=True)
    return full.reshape(-1, full.shape[-1])


def scatter_dp(grad):
    return lax.psum_scatter(grad, "dp", scatter_dimension=grad.ndim - 2, tiled=True)


def all_small(vectors):
    count = lax.axis_size("seq") * lax.axis_size("dp")
    packed = jnp.concatenate(vectors)
    table = lax.all_to_all(jnp.broadcast_to(packed[None], (count, packed.shape[0])), ALL, 0, 0)
    out = []
    start = 0
    for vector in vectors:
        size = vector.shape[0]
        out.append(table[:, start : start + size].reshape(-1).astype(f32))
        start += size
    return out


def scatter_small(vectors):
    count = lax.axis_size("seq") * lax.axis_size("dp")
    packed = jnp.concatenate([v.reshape(count, -1) for v in vectors], axis=1)
    mine = jnp.sum(lax.all_to_all(packed, ALL, 0, 0), axis=0)
    out = []
    start = 0
    for vector in vectors:
        size = vector.shape[0] // count
        out.append(mine[start : start + size])
        start += size
    return out


def gelu_parts(v):
    c = 0.7978845608028654
    t = jnp.tanh(c * (v + 0.044715 * v * v * v))
    value = 0.5 * v * (1.0 + t)
    slope = 0.5 * (1.0 + t) + 0.5 * v * (1.0 - t * t) * c * (1.0 + 3 * 0.044715 * v * v)
    return value, slope


def per_device(
    tokens,
    doc_lengths,
    qkv_weight,
    qv_bias,
    out_weight,
    out_bias,
    norm1_gain,
    norm1_bias,
    in_weight,
    in_bias,
    down_weight,
    down_bias,
    norm2_gain,
    norm2_bias,
    cotangent,
):
    n = lax.axis_size("seq")
    groups = lax.axis_size("dp")
    s = lax.axis_index("seq")
    rows = tokens.shape[1]
    width = tokens.shape[2]
    part = width // n
    tok_rows = tokens[0]
    ends = jnp.cumsum(doc_lengths[0])
    steps = jnp.arange(n * rows, dtype=jnp.int32)
    places = jnp.remainder(s - steps // rows, n) * rows + steps % rows
    seg = jnp.sum((places[:, None] >= ends[None, :]).astype(jnp.int32), axis=1)

    small = all_small(
        [qv_bias, out_bias, norm1_gain, norm1_bias, in_bias, down_bias, norm2_gain, norm2_bias]
    )
    qv_full, out_b, gain_one, shift_one, in_b, down_b, gain_two, shift_two = small
    out_w = gather_dp(out_weight)
    qkv_packed = pack_columns(qkv_weight, 3)
    qkv_moved = join_rows(exchange(qkv_packed))
    qkv_w = gather_dp(after(qkv_moved, out_w, small))
    tok_blocks = gather_blocks(after(tok_rows, qkv_packed))
    tok_full = jnp.concatenate(tok_blocks, axis=0)
    down_w = gather_dp(after(down_weight, qkv_moved))
    in_packed = after(pack_columns(in_weight, 1), tok_blocks)
    in_blocks = exchange(in_packed)

    q_bias = lax.dynamic_slice_in_dim(qv_full, s * part, part)
    v_bias = lax.dynamic_slice_in_dim(qv_full, width + s * part, part)
    qkv_b = jnp.concatenate([q_bias, jnp.zeros((part,), f32), v_bias])
    qkv = (dot_nn(tok_full, qkv_w) + qkv_b).astype(bf16)
    mixed = attend(qkv, seg)
    in_blocks, mixed = lax.optimization_barrier((in_blocks, mixed))
    in_w = gather_dp(join_rows(in_blocks))
    attn = scatter_seq(dot_nn(mixed, out_w)) + out_b
    normed_one, recip_one = normalize(tok_rows.astype(f32) + attn)
    first = normed_one * gain_one + shift_one
    first_full = gather_seq(first.astype(bf16))
    hidden = in_w.shape[1]
    pre = dot_nn(first_full, in_w) + lax.dynamic_slice_in_dim(in_b, s * hidden, hidden)
    act_value, act_slope = gelu_parts(pre)
    act, act_slope = lax.optimization_barrier((act_value.astype(bf16), act_slope.astype(bf16)))
    ffn = scatter_seq(dot_nn(act, down_w)) + down_b
    normed_two, recip_two = normalize(first + ffn)
    result = (normed_two * gain_two + shift_two).astype(bf16)

    grad_out = cotangent[0].astype(f32)
    shift_two_grad = jnp.sum(grad_out, axis=0)
    gain_two_grad = jnp.sum(grad_out * normed_two, axis=0)
    grad_h2 = norm_back(grad_out, normed_two, recip_two, gain_two)
    grad_ffn = grad_h2.astype(bf16)
    down_b_grad = jnp.sum(grad_ffn.astype(f32), axis=0)
    grad_ffn_full = gather_seq(grad_ffn)
    grad_pre = (dot_nt(grad_ffn_full, down_w) * act_slope.astype(f32)).astype(bf16)
    back_blocks = scatter_blocks(dot_nt(grad_pre, in_w))
    in_b_grad = jnp.sum(grad_pre.astype(f32), axis=0)
    merge = down_w.shape[0] == width
    if merge:
        low = feed_grads(n, groups, act, grad_ffn_full, first_full, grad_pre)
    else:
        down_low = dot_tn(act, grad_ffn_full).astype(bf16)
        low = (down_low, dot_tn(first_full, grad_pre).astype(bf16).reshape(n, part, -1))
    back_blocks, low = lax.optimization_barrier((back_blocks, low))
    grad_first = grad_h2 + total_of(back_blocks)
    if merge:
        mine = scatter_dp(low)
        down_mine = mine[:n].reshape(-1, width)
        in_mine = mine[n:]
    else:
        down_mine = scatter_dp(low[0])
        in_mine = scatter_dp(low[1])

    shift_one_grad = jnp.sum(grad_first, axis=0)
    gain_one_grad = jnp.sum(grad_first * normed_one, axis=0)
    grad_h1 = norm_back(grad_first, normed_one, recip_one, gain_one)
    grad_attn = grad_h1.astype(bf16)
    out_b_grad = jnp.sum(grad_attn.astype(f32), axis=0)
    grad_attn_full = gather_seq(grad_attn)
    grad_mixed = dot_nt(grad_attn_full, out_w).astype(bf16)
    grad_qkv = attend_back(qkv, grad_mixed, seg)
    last_blocks = scatter_blocks(dot_nt(grad_qkv, qkv_w))
    attn_low = attn_grads(n, tok_full, grad_qkv, mixed, grad_attn_full)
    attn_mine = scatter_dp(after(attn_low, in_mine))
    input_grad = (grad_h1 + total_of(last_blocks)).astype(bf16)
    down_w_grad = down_mine.astype(f32)
    in_w_grad = join_columns(exchange_back(in_mine), 1)
    out_w_grad = jnp.concatenate([attn_mine[j, :, 3 * part :] for j in range(n)], 1).astype(f32)
    qkv_w_grad = join_columns(exchange_back(attn_mine[:, :, : 3 * part]), 3)

    sums = jnp.sum(grad_qkv.astype(f32), axis=0)
    qv_grad = jnp.zeros((2 * width,), f32)
    qv_grad = lax.dynamic_update_slice_in_dim(qv_grad, sums[:part], s * part, 0)
    qv_grad = lax.dynamic_update_slice_in_dim(qv_grad, sums[2 * part :], width + s * part, 0)
    in_b_all = jnp.zeros((n * hidden,), f32)
    in_b_all = lax.dynamic_update_slice_in_dim(in_b_all, in_b_grad, s * hidden, 0)
    small_grads = scatter_small(
        [
            qv_grad,
            out_b_grad,
            gain_one_grad,
            shift_one_grad,
            in_b_all,
            down_b_grad,
            gain_two_grad,
            shift_two_grad,
        ]
    )
    return (
        result[None],
        input_grad[None],
        qkv_w_grad,
        small_grads[0],
        out_w_grad,
        small_grads[1],
        small_grads[2],
        small_grads[3],
        in_w_grad,
        small_grads[4],
        down_w_grad,
        small_grads[5],
        small_grads[6],
        small_grads[7],
    )


def solution(mesh):
    rows = P(("seq", "dp"), None)
    flat = P(("seq", "dp"))
    tok = P("dp", "seq", None)
    return jax.shard_map(
        per_device,
        mesh=mesh,
        in_specs=(
            tok,
            P("dp", None),
            rows,
            flat,
            rows,
            flat,
            flat,
            flat,
            rows,
            flat,
            rows,
            flat,
            flat,
            flat,
            tok,
        ),
        out_specs=(tok, tok, rows, flat, rows, flat, flat, flat, rows, flat, rows, flat, flat, flat),
        check_vma=False,
    )
```

```python
import jax
import jax.numpy as jnp
from jax import lax
from jax.experimental import pallas as pl
from jax.experimental.pallas import tpu as pltpu
from jax.sharding import PartitionSpec as P

HEAD_DIM = 128
eps_norm = 1e-06
f32 = jnp.float32
bf16 = jnp.bfloat16
DP = ("chip", "core")
ALL = ("seq", "chip", "core")


def after(value, *others):
    return lax.optimization_barrier((value, *others))[0]


def shift(value, step):
    n = lax.axis_size("seq")
    return lax.ppermute(value, "seq", [(i, (i + step) % n) for i in range(n)])


def gather_blocks(rows):
    n = lax.axis_size("seq")
    return [rows] + [shift(rows, k) for k in range(1, n)]


def gather_seq(rows):
    return jnp.concatenate(gather_blocks(rows), axis=0)


def split_blocks(partial, part=0, parts=1):
    n = lax.axis_size("seq")
    size = partial.shape[0] // (n * parts)
    starts = [(k * parts + part) * size for k in range(n)]
    blocks = [partial[start : start + size] for start in starts]
    return [blocks[0]] + [block.astype(bf16) for block in blocks[1:]]


def send_blocks(blocks):
    return [blocks[0]] + [shift(blocks[k], -k) for k in range(1, len(blocks))]


def total_of(blocks):
    total = blocks[0]
    for block in blocks[1:]:
        total = total + block.astype(f32)
    return total


def scatter_seq(partial):
    return total_of(send_blocks(split_blocks(partial)))


def normalize(hidden):
    center = hidden - jnp.mean(hidden, axis=-1, keepdims=True)
    spread = jnp.mean(center * center, axis=-1, keepdims=True)
    recip = lax.rsqrt(spread + eps_norm)
    return (center * recip, recip)


def norm_back(grad_out, normed, recip, gain):
    scaled = grad_out * gain
    return recip * (
        scaled
        - jnp.mean(scaled, axis=-1, keepdims=True)
        - normed * jnp.mean(scaled * normed, axis=-1, keepdims=True)
    )


def dot_nn(a, b):
    return lax.dot_general(a, b, (((1,), (0,)), ((), ())), preferred_element_type=f32)


def dot_nt(a, b):
    return lax.dot_general(a, b, (((1,), (1,)), ((), ())), preferred_element_type=f32)


def dot_tn(a, b):
    return lax.dot_general(a, b, (((0,), (0,)), ((), ())), preferred_element_type=f32)


def grid_call(kernel, scalar, grid, in_specs, out_specs, out_shape, name, args, flops=None):
    grid_spec = pltpu.PrefetchScalarGridSpec(
        num_scalar_prefetch=1, grid=grid, in_specs=in_specs, out_specs=out_specs
    )
    return pl.pallas_call(
        kernel,
        grid_spec=grid_spec,
        out_shape=out_shape,
        compiler_params=pltpu.CompilerParams(vmem_limit_bytes=56 << 20),
        cost_estimate=flops and pl.CostEstimate(flops=flops, transcendentals=0, bytes_accessed=1),
        name=name,
    )(jnp.reshape(scalar, (1,)).astype(jnp.int32), *args)


def fixed(shape):
    return pl.BlockSpec(shape, lambda g, sc: (0,) * len(shape))


def softmax_of(q, k, seg_col, seg_row):
    scores = dot_nt(q, k) * HEAD_DIM ** (-0.5)
    scores = jnp.where(seg_col == seg_row, scores, -1e30)
    terms = jnp.exp(scores - jnp.max(scores, axis=1, keepdims=True))
    return terms / jnp.sum(terms, axis=1, keepdims=True)


def attend_kernel(core, seg_col, seg_row, q, k, v, mixed):
    probs = softmax_of(q[...], k[...], seg_col[...], seg_row[...])
    mixed[...] = dot_nn(probs.astype(bf16), v[...]).astype(bf16)


def attend_back_kernel(core, seg_col, seg_row, q, k, v, gm, grad, sent):
    heads = pl.num_programs(0)
    head = pl.program_id(0)
    probs = softmax_of(q[...], k[...], seg_col[...], seg_row[...])
    grad_probs = dot_nt(gm[...], v[...])
    products = jnp.sum(probs * grad_probs, axis=1, keepdims=True)
    grad_scores = (probs * (grad_probs - products)).astype(bf16)
    scale = HEAD_DIM ** (-0.5)
    half = heads // 2

    def put(part, value):
        value = value.astype(bf16)
        start = pl.multiple_of((part * heads + head) * HEAD_DIM, HEAD_DIM)
        grad[:, pl.ds(start, HEAD_DIM)] = value

        @pl.when(head // half != core[0])
        def _():
            into = pl.multiple_of((part * half + head % half) * HEAD_DIM, HEAD_DIM)
            sent[:, pl.ds(into, HEAD_DIM)] = value

    put(0, dot_nn(grad_scores, k[...]) * scale)
    put(1, dot_tn(grad_scores, q[...]) * scale)
    put(2, dot_tn(probs.astype(bf16), gm[...]))


def head_spec(rows, offset):
    return pl.BlockSpec((rows, HEAD_DIM), lambda h, sc: (0, offset + h))


def qkv_specs(rows, heads):
    return [
        fixed((rows, 1)),
        fixed((1, rows)),
        head_spec(rows, 0),
        head_spec(rows, heads),
        head_spec(rows, 2 * heads),
    ]


def attend(qkv, seg, core):
    rows, width = qkv.shape
    heads = width // (3 * HEAD_DIM)
    return grid_call(
        attend_kernel,
        core,
        (heads,),
        qkv_specs(rows, heads),
        head_spec(rows, 0),
        jax.ShapeDtypeStruct((rows, width // 3), bf16),
        "attend",
        (seg[:, None], seg[None, :], qkv, qkv, qkv),
    )


def attend_back(qkv, grad_mixed, seg, core):
    rows, width = qkv.shape
    heads = width // (3 * HEAD_DIM)
    return grid_call(
        attend_back_kernel,
        core,
        (heads,),
        qkv_specs(rows, heads) + [head_spec(rows, 0)],
        [fixed((rows, width)), fixed((rows, width // 2))],
        [
            jax.ShapeDtypeStruct((rows, width), bf16),
            jax.ShapeDtypeStruct((rows, width // 2), bf16),
        ],
        "attend_back",
        (seg[:, None], seg[None, :], qkv, qkv, qkv, grad_mixed),
        flops=400_000_000_000,
    )


def pack_columns(shard, parts, core):
    n = lax.axis_size("seq")
    rows, width = shard.shape
    part = width // (parts * n)

    def kernel(sc, shard_ref, out):
        for j in range(n):
            for p in range(parts):
                start = (p * n + j) * part
                out[j, :, p * part : (p + 1) * part] = shard_ref[:, start : start + part]

    out = (n, rows, part * parts)
    return grid_call(
        kernel,
        core,
        (1,),
        [fixed(shard.shape)],
        fixed(out),
        jax.ShapeDtypeStruct(out, shard.dtype),
        "pack",
        (shard,),
    )


def join_columns(pieces, parts, halves, core):
    n, rows, width = pieces.shape
    piece = width // (parts * halves)

    def kernel(sc, pieces_ref, out):
        for h in range(halves):
            for j in range(n):
                for p in range(parts):
                    start = (p * n + j) * halves * piece
                    if halves > 1:
                        side = jnp.bitwise_xor(sc[0], h)
                        start = pl.multiple_of(start + side * piece, piece)
                    at = (h * parts + p) * piece
                    value = pieces_ref[j, :, at : at + piece].astype(f32)
                    out[:, pl.ds(start, piece)] = value

    out = (rows, n * width)
    return grid_call(
        kernel,
        core,
        (1,),
        [fixed(pieces.shape)],
        fixed(out),
        jax.ShapeDtypeStruct(out, f32),
        "join_columns",
        (pieces,),
    )


def exchange(pieces):
    return lax.all_to_all(pieces, "seq", 0, 0)


def gather_dp(shard):
    full = lax.all_gather(shard, DP, axis=shard.ndim - 2, tiled=True)
    return full.reshape(-1, full.shape[-1])


def sum_over(value, axes):
    return lax.psum_scatter(value, axes, scatter_dimension=value.ndim - 2, tiled=True)


def to_partner(value):
    return lax.ppermute(value, "core", [(0, 1), (1, 0)])


def column_half(value, index):
    width = value.shape[1] // 2
    return lax.dynamic_slice_in_dim(value, index * width, width, axis=1)


def feed_grad(core, own, far, grad_own, grad_far, name):
    tokens, height = own.shape
    width = grad_far.shape[1]
    rows = 256

    def kernel(sc, a, b, go, gf, out):
        out[...] = (dot_tn(a[...], go[...]) + dot_tn(b[...], gf[...])).astype(bf16)

    rows_spec = pl.BlockSpec((tokens, rows), lambda g, sc: (0, g))
    return grid_call(
        kernel,
        core,
        (height // rows,),
        [
            rows_spec,
            rows_spec,
            pl.BlockSpec((tokens, width), lambda g, sc: (0, sc[0])),
            fixed((tokens, width)),
        ],
        pl.BlockSpec((rows, width), lambda g, sc: (g, 0)),
        jax.ShapeDtypeStruct((height, width), bf16),
        name,
        (own, far, grad_own, grad_far),
        flops=1,
    )


def attn_grad(core, tok, tok_far, mixed, mixed_far, grad_qkv, qkv_far, grad_attn, attn_far):
    n = lax.axis_size("seq")
    chips = lax.axis_size("chip")
    tokens = tok.shape[0]
    half = qkv_far.shape[1] // 3
    out_cols = attn_far.shape[1]
    cols = out_cols // n
    rows = mixed.shape[1] // chips

    def kernel(sc, *refs):
        own_refs, far_refs = refs[:n], refs[n : 2 * n]
        mo, mf, qo, ko, vo, qkv_f, ao, af, out = refs[2 * n :]
        side = (dot_tn(mo[...], ao[...]) + dot_tn(mf[...], af[...])).astype(bf16)
        own = jnp.concatenate([qo[...], ko[...], vo[...]], axis=1)
        for j in range(n):
            total = dot_tn(own_refs[j][...], own) + dot_tn(far_refs[j][...], qkv_f[...])
            out[j, :, : 3 * half] = total.astype(bf16)
            out[j, :, 3 * half :] = side[:, j * cols : (j + 1) * cols]

    def rows_spec(j):
        return pl.BlockSpec((tokens, rows), lambda o, sc: (0, j * chips + o))

    def part_spec(p):
        return pl.BlockSpec((tokens, half), lambda o, sc: (0, 2 * p + sc[0]))

    width = 3 * half + cols
    return grid_call(
        kernel,
        core,
        (chips,),
        [rows_spec(j) for j in range(n)] * 2
        + [rows_spec(0)] * 2
        + [part_spec(p) for p in range(3)]
        + [
            fixed((tokens, 3 * half)),
            pl.BlockSpec((tokens, out_cols), lambda o, sc: (0, sc[0])),
            fixed((tokens, out_cols)),
        ],
        pl.BlockSpec((n, rows, width), lambda o, sc: (0, o, 0)),
        jax.ShapeDtypeStruct((n, chips * rows, width), bf16),
        "attn_grad",
        (
            *[tok] * n,
            *[tok_far] * n,
            mixed,
            mixed_far,
            *[grad_qkv] * 3,
            qkv_far,
            grad_attn,
            attn_far,
        ),
    )


def pick(value, axis, index):
    return lax.dynamic_index_in_dim(value, index, axis, keepdims=False)


def swap_rows(total, split, axis, core):
    value = total.reshape(split)
    return pick(value, axis, core), to_partner(pick(value, axis, 1 - core).astype(bf16))


def join_halves(own, far, core):
    return jnp.where(
        core == 0, jnp.concatenate([own, far], axis=-1), jnp.concatenate([far, own], axis=-1)
    )


def device_count():
    return lax.axis_size("seq") * lax.axis_size("chip") * lax.axis_size("core")


def all_small(vectors):
    count = device_count()
    packed = jnp.concatenate(vectors)
    table = lax.all_to_all(jnp.broadcast_to(packed[None], (count, packed.shape[0])), ALL, 0, 0)
    out = []
    start = 0
    for vector in vectors:
        size = vector.shape[0]
        out.append(table[:, start : start + size].reshape(-1).astype(f32))
        start += size
    return out


def scatter_small(vectors):
    count = device_count()
    packed = jnp.concatenate([v.reshape(count, -1) for v in vectors], axis=1)
    mine = jnp.sum(lax.all_to_all(packed, ALL, 0, 0), axis=0)
    out = []
    start = 0
    for vector in vectors:
        size = vector.shape[0] // count
        out.append(mine[start : start + size])
        start += size
    return out


def gelu_parts(v):
    c = 0.7978845608028654
    t = jnp.tanh(c * (v + 0.044715 * v * v * v))
    value = 0.5 * v * (1.0 + t)
    slope = 0.5 * (1.0 + t) + 0.5 * v * (1.0 - t * t) * c * (1.0 + 3 * 0.044715 * v * v)
    return value, slope


def per_device(
    tokens,
    doc_lengths,
    qkv_weight,
    qv_bias,
    out_weight,
    out_bias,
    norm1_gain,
    norm1_bias,
    in_weight,
    in_bias,
    down_weight,
    down_bias,
    norm2_gain,
    norm2_bias,
    cotangent,
):
    n = lax.axis_size("seq")
    chips = lax.axis_size("chip")
    s = lax.axis_index("seq")
    c = lax.axis_index("core")
    rows = tokens.shape[1]
    width = tokens.shape[2]
    part = width // n
    half = width // 2
    paired = part // chips % 128 == 0
    tok_rows = tokens[0]

    tok_blocks = gather_blocks(tok_rows)
    tok_full = jnp.concatenate(tok_blocks, axis=0)
    out_w = gather_dp(out_weight)
    qkv_moved = exchange(pack_columns(qkv_weight, 3, c))
    vectors = [qv_bias, out_bias, norm1_gain, norm1_bias]
    vectors += [in_bias, down_bias, norm2_gain, norm2_bias]
    small = all_small(after(vectors, qkv_moved))
    qv_full, out_b, gain_one, shift_one, in_b, down_b, gain_two, shift_two = small
    qkv_w = gather_dp(after(qkv_moved, out_w, tok_blocks[1]))
    in_moved = exchange(after(pack_columns(in_weight, 1, c), tok_blocks))
    down_w = gather_dp(after(down_weight, qkv_moved))

    ends = jnp.cumsum(doc_lengths[0])
    steps = jnp.arange(n * rows, dtype=jnp.int32)
    places = jnp.remainder(s - steps // rows, n) * rows + steps % rows
    seg = jnp.sum((places[:, None] >= ends[None, :]).astype(jnp.int32), axis=1)

    q_bias = lax.dynamic_slice_in_dim(qv_full, s * part, part)
    v_bias = lax.dynamic_slice_in_dim(qv_full, width + s * part, part)
    qkv_b = jnp.concatenate([q_bias, jnp.zeros((part,), f32), v_bias])
    qkv = (dot_nn(tok_full, qkv_w) + qkv_b).astype(bf16)
    mixed = attend(qkv, seg, c)
    size = rows // 2
    halves = range(2)
    cut = [slice(h * size, (h + 1) * size) for h in halves]
    attn_partial = dot_nn(mixed, out_w)
    attn_blocks = [send_blocks(split_blocks(attn_partial, h, 2)) for h in halves]
    in_w = gather_dp(after(in_moved, attn_blocks[0], down_w))
    hidden = in_w.shape[1]
    in_bias_own = lax.dynamic_slice_in_dim(in_b, s * hidden, hidden)

    first, normed_one, recip_one, first_blocks = [], [], [], []
    for h in halves:
        if h:
            attn_blocks[h] = after(attn_blocks[h], first[0])
        attn = total_of(attn_blocks[h]) + out_b
        normed, recip = normalize(tok_rows[cut[h]].astype(f32) + attn)
        normed_one.append(normed)
        recip_one.append(recip)
        first.append(normed * gain_one + shift_one)
        first_blocks.append(gather_blocks(first[h].astype(bf16)))

    first_blocks[0] = after(first_blocks[0], first[1])
    act, act_slope, first_full, ffn_blocks, ffn_split = [], [], [], [], []
    for h in halves:
        if h:
            first_blocks[h] = after(first_blocks[h], ffn_split[0])
        first_full.append(jnp.concatenate(first_blocks[h], axis=0))
        act_value, slope = gelu_parts(dot_nn(first_full[h], in_w) + in_bias_own)
        pair = lax.optimization_barrier((act_value.astype(bf16), slope.astype(bf16)))
        act.append(pair[0])
        act_slope.append(pair[1])
        ffn_split.append(split_blocks(dot_nn(act[h], down_w)))
        ffn_blocks.append(send_blocks(ffn_split[h]))

    ffn_blocks[0] = after(ffn_blocks[0], ffn_split[1])
    result, normed_two, grad_h2, grad_ffn, grad_blocks = [], [], [], [], []
    grad_out = cotangent[0].astype(f32)
    for h in halves:
        if h:
            ffn_blocks[h] = after(ffn_blocks[h], grad_ffn[0])
        ffn = total_of(ffn_blocks[h]) + down_b
        normed, recip = normalize(first[h] + ffn)
        normed_two.append(normed)
        result.append((normed * gain_two + shift_two).astype(bf16))
        grad_h2.append(norm_back(grad_out[cut[h]], normed, recip, gain_two))
        grad_ffn.append(grad_h2[h].astype(bf16))
        grad_blocks.append(gather_blocks(grad_ffn[h]))
    result = jnp.concatenate(result, axis=0)
    shift_two_grad = jnp.sum(grad_out, axis=0)
    gain_two_grad = sum(jnp.sum(grad_out[cut[h]] * normed_two[h], axis=0) for h in halves)
    down_b_grad = sum(jnp.sum(grad_ffn[h].astype(f32), axis=0) for h in halves)

    grad_blocks[0] = after(grad_blocks[0], grad_ffn[1])
    grad_ffn_full, grad_pre, back_split, back_blocks = [], [], [], []
    for h in halves:
        if h:
            grad_blocks[h] = after(grad_blocks[h], back_split[0])
        grad_ffn_full.append(jnp.concatenate(grad_blocks[h], axis=0))
        grad_act = dot_nt(grad_ffn_full[h], down_w)
        grad_pre.append((grad_act * act_slope[h].astype(f32)).astype(bf16))
        back_split.append(split_blocks(dot_nt(grad_pre[h], in_w)))
        back_blocks.append(send_blocks(back_split[h]))
    act, first_full, grad_ffn_full, grad_pre = (
        jnp.concatenate(v, axis=0) for v in (act, first_full, grad_ffn_full, grad_pre)
    )
    in_b_grad = jnp.sum(grad_pre.astype(f32), axis=0)
    back_blocks[0] = after(back_blocks[0], back_split[1])
    if paired:
        tok_far, mixed_far, first_far, act_far = (
            to_partner(v) for v in (tok_full, mixed, first_full, act)
        )
        ffn_far = to_partner(column_half(grad_ffn_full, 1 - c))
        pre_far = to_partner(column_half(grad_pre, 1 - c))
        at = after(c, back_split[1])
        in_low = feed_grad(at, first_full, first_far, grad_pre, pre_far, "in_grad")
        back_blocks[1], in_low = lax.optimization_barrier((back_blocks[1], in_low))
        in_sum = sum_over(in_low.reshape(n, part, -1), "chip")
    else:
        down_low = dot_tn(act, grad_ffn_full).astype(bf16)
        in_low = dot_tn(first_full, grad_pre).astype(bf16).reshape(n, part, -1)
        down_w_grad = sum_over(down_low, DP).astype(f32)
        in_w_grad = join_columns(exchange(sum_over(in_low, DP)), 1, 1, c)
    grad_first, grad_h1, grad_attn, attn_blocks = [], [], [], []
    for h in halves:
        if h:
            back_blocks[h] = after(back_blocks[h], grad_attn[0])
        grad_first.append(grad_h2[h] + total_of(back_blocks[h]))
        grad_h1.append(norm_back(grad_first[h], normed_one[h], recip_one[h], gain_one))
        grad_attn.append(grad_h1[h].astype(bf16))
        attn_blocks.append(gather_blocks(grad_attn[h]))
    if paired:
        at = after(c, grad_attn[1])
        down_low = feed_grad(at, act, act_far, grad_ffn_full, ffn_far, "down_grad")
        down_got = lax.all_to_all(down_low.reshape(chips, -1, half), "chip", 0, 0)
    attn_blocks = after(attn_blocks, down_low)
    shift_one_grad = sum(jnp.sum(grad_first[h], axis=0) for h in halves)
    gain_one_grad = sum(jnp.sum(grad_first[h] * normed_one[h], axis=0) for h in halves)
    out_b_grad = sum(jnp.sum(grad_attn[h].astype(f32), axis=0) for h in halves)
    grad_h1 = jnp.concatenate(grad_h1, axis=0)
    grad_attn_full = jnp.concatenate([attn_blocks[h][k] for k in range(n) for h in halves], axis=0)
    grad_mixed = dot_nt(grad_attn_full, out_w).astype(bf16)
    grad_qkv, qkv_sent = attend_back(qkv, grad_mixed, seg, c)
    if paired:
        attn_far = to_partner(column_half(grad_attn_full, 1 - c))
        in_own, in_far = swap_rows(after(in_sum, qkv_sent), (n, 2, -1, half), 1, c)
        in_pieces = exchange(jnp.concatenate([in_own, in_far], axis=2))
        args = (tok_full, tok_far, mixed, mixed_far)
        qkv_far = to_partner(qkv_sent)
        attn_low = attn_grad(c, *args, grad_qkv, qkv_far, grad_attn_full, attn_far)
        attn_sum = sum_over(attn_low, "chip")
        last_split = split_blocks(dot_nt(after(grad_qkv, attn_low), qkv_w))
        last_blocks = send_blocks(last_split)
        down_sum = jnp.sum(after(down_got, last_split).astype(f32), axis=0)
        down_own, down_far = swap_rows(down_sum, (2, -1, half), 0, c)
        down_w_grad = join_halves(down_own, down_far.astype(f32), c)
        in_w_grad = join_columns(in_pieces, 1, 2, c)
        attn_sum = after(attn_sum, last_blocks)
        attn_own, attn_far = swap_rows(attn_sum, (n, 2, -1, half), 1, c)
        split = 3 * part // 2
        pieces = jnp.concatenate([attn_own[:, :, :split], attn_far[:, :, :split]], 2)
        qkv_w_grad = join_columns(exchange(pieces), 3, 2, c)
        out_own, out_far = (
            jnp.concatenate([v[j, :, split:] for j in range(n)], axis=1).astype(f32)
            for v in (attn_own, attn_far)
        )
        out_w_grad = join_halves(out_own, out_far, c)
    else:
        last_split = split_blocks(dot_nt(grad_qkv, qkv_w))
        last_blocks = send_blocks(last_split)
        attn_low = after(dot_tn(tok_full, grad_qkv).astype(bf16), last_split)
        out_w_grad = sum_over(dot_tn(mixed, grad_attn_full).astype(bf16), DP).astype(f32)
        pieces = exchange(sum_over(attn_low.reshape(n, part, -1), DP))
        qkv_w_grad = join_columns(pieces, 3, 1, c)
    sums = jnp.sum(grad_qkv.astype(f32), axis=0)
    qv_grad = jnp.zeros((2 * width,), f32)
    qv_grad = lax.dynamic_update_slice_in_dim(qv_grad, sums[:part], s * part, 0)
    qv_grad = lax.dynamic_update_slice_in_dim(qv_grad, sums[2 * part :], width + s * part, 0)
    in_b_all = jnp.zeros((n * hidden,), f32)
    in_b_all = lax.dynamic_update_slice_in_dim(in_b_all, in_b_grad, s * hidden, 0)
    small_grads = scatter_small(
        [
            qv_grad,
            out_b_grad,
            gain_one_grad,
            shift_one_grad,
            in_b_all,
            down_b_grad,
            gain_two_grad,
            shift_two_grad,
        ]
    )
    last_blocks = after(last_blocks, small_grads)
    input_grad = (grad_h1 + total_of(last_blocks)).astype(bf16)
    return (
        result[None],
        input_grad[None],
        qkv_w_grad,
        small_grads[0],
        out_w_grad,
        small_grads[1],
        small_grads[2],
        small_grads[3],
        in_w_grad,
        small_grads[4],
        down_w_grad,
        small_grads[5],
        small_grads[6],
        small_grads[7],
    )


def solution(mesh):
    devices = mesh.devices
    split = jax.sharding.Mesh(devices.reshape(devices.shape[0], -1, 2), ALL)
    rows = P(ALL, None)
    flat = P(ALL)
    tok = P(DP, "seq", None)
    ins = (tok, P(DP, None), rows, flat, rows, *[flat] * 3, rows, flat, rows, *[flat] * 3, tok)
    outs = (tok, tok, rows, flat, rows, *[flat] * 3, rows, flat, rows, *[flat] * 3)
    return jax.shard_map(per_device, mesh=split, in_specs=ins, out_specs=outs, check_vma=False)
```

```python
import jax
import jax.numpy as jnp
from jax import lax
from jax.experimental import pallas as pl
from jax.experimental.pallas import tpu as pltpu
from jax.sharding import PartitionSpec as P

HEAD_DIM = 128
eps_norm = 1e-06
f32 = jnp.float32
bf16 = jnp.bfloat16
DP = ("chip", "core")
ALL = ("seq", "chip", "core")


def after(value, *others):
    return lax.optimization_barrier((value, *others))[0]


def shift(value, step):
    n = lax.axis_size("seq")
    return lax.ppermute(value, "seq", [(i, (i + step) % n) for i in range(n)])


def gather_blocks(rows):
    n = lax.axis_size("seq")
    return [rows] + [shift(rows, k) for k in range(1, n)]


def gather_seq(rows):
    return jnp.concatenate(gather_blocks(rows), axis=0)


def split_blocks(partial, part=0, parts=1):
    n = lax.axis_size("seq")
    size = partial.shape[0] // (n * parts)
    starts = [(k * parts + part) * size for k in range(n)]
    blocks = [partial[start : start + size] for start in starts]
    return [blocks[0]] + [block.astype(bf16) for block in blocks[1:]]


def send_blocks(blocks):
    return [blocks[0]] + [shift(blocks[k], -k) for k in range(1, len(blocks))]


def total_of(blocks):
    total = blocks[0]
    for block in blocks[1:]:
        total = total + block.astype(f32)
    return total


def scatter_seq(partial):
    return total_of(send_blocks(split_blocks(partial)))


def normalize(hidden):
    center = hidden - jnp.mean(hidden, axis=-1, keepdims=True)
    spread = jnp.mean(center * center, axis=-1, keepdims=True)
    recip = lax.rsqrt(spread + eps_norm)
    return (center * recip, recip)


def norm_back(grad_out, normed, recip, gain):
    scaled = grad_out * gain
    return recip * (
        scaled
        - jnp.mean(scaled, axis=-1, keepdims=True)
        - normed * jnp.mean(scaled * normed, axis=-1, keepdims=True)
    )


def dot_nn(a, b):
    return lax.dot_general(a, b, (((1,), (0,)), ((), ())), preferred_element_type=f32)


def dot_nt(a, b):
    return lax.dot_general(a, b, (((1,), (1,)), ((), ())), preferred_element_type=f32)


def dot_tn(a, b):
    return lax.dot_general(a, b, (((0,), (0,)), ((), ())), preferred_element_type=f32)


def grid_call(kernel, scalar, grid, in_specs, out_specs, out_shape, name, args, flops=None):
    grid_spec = pltpu.PrefetchScalarGridSpec(
        num_scalar_prefetch=1, grid=grid, in_specs=in_specs, out_specs=out_specs
    )
    return pl.pallas_call(
        kernel,
        grid_spec=grid_spec,
        out_shape=out_shape,
        compiler_params=pltpu.CompilerParams(vmem_limit_bytes=56 << 20),
        cost_estimate=flops and pl.CostEstimate(flops=flops, transcendentals=0, bytes_accessed=1),
        name=name,
    )(jnp.reshape(scalar, (1,)).astype(jnp.int32), *args)


def fixed(shape):
    return pl.BlockSpec(shape, lambda g, sc: (0,) * len(shape))


def softmax_of(q, k, seg_col, seg_row):
    scores = dot_nt(q, k) * HEAD_DIM ** (-0.5)
    scores = jnp.where(seg_col == seg_row, scores, -1e30)
    terms = jnp.exp(scores - jnp.max(scores, axis=1, keepdims=True))
    return terms / jnp.sum(terms, axis=1, keepdims=True)


def attend_kernel(core, seg_col, seg_row, q, k, v, mixed):
    probs = softmax_of(q[...], k[...], seg_col[...], seg_row[...])
    mixed[...] = dot_nn(probs.astype(bf16), v[...]).astype(bf16)


def attend_back_kernel(core, seg_col, seg_row, q, k, v, gm, grad, sent):
    heads = pl.num_programs(0)
    head = pl.program_id(0)
    probs = softmax_of(q[...], k[...], seg_col[...], seg_row[...])
    grad_probs = dot_nt(gm[...], v[...])
    products = jnp.sum(probs * grad_probs, axis=1, keepdims=True)
    grad_scores = (probs * (grad_probs - products)).astype(bf16)
    scale = HEAD_DIM ** (-0.5)
    half = heads // 2

    def put(part, value):
        value = value.astype(bf16)
        start = pl.multiple_of((part * heads + head) * HEAD_DIM, HEAD_DIM)
        grad[:, pl.ds(start, HEAD_DIM)] = value

        @pl.when(head // half != core[0])
        def _():
            into = pl.multiple_of((part * half + head % half) * HEAD_DIM, HEAD_DIM)
            sent[:, pl.ds(into, HEAD_DIM)] = value

    put(0, dot_nn(grad_scores, k[...]) * scale)
    put(1, dot_tn(grad_scores, q[...]) * scale)
    put(2, dot_tn(probs.astype(bf16), gm[...]))


def head_spec(rows, offset):
    return pl.BlockSpec((rows, HEAD_DIM), lambda h, sc: (0, offset + h))


def qkv_specs(rows, heads):
    return [
        fixed((rows, 1)),
        fixed((1, rows)),
        head_spec(rows, 0),
        head_spec(rows, heads),
        head_spec(rows, 2 * heads),
    ]


def attend(qkv, seg, core):
    rows, width = qkv.shape
    heads = width // (3 * HEAD_DIM)
    return grid_call(
        attend_kernel,
        core,
        (heads,),
        qkv_specs(rows, heads),
        head_spec(rows, 0),
        jax.ShapeDtypeStruct((rows, width // 3), bf16),
        "attend",
        (seg[:, None], seg[None, :], qkv, qkv, qkv),
    )


def attend_back(qkv, grad_mixed, seg, core):
    rows, width = qkv.shape
    heads = width // (3 * HEAD_DIM)
    return grid_call(
        attend_back_kernel,
        core,
        (heads,),
        qkv_specs(rows, heads) + [head_spec(rows, 0)],
        [fixed((rows, width)), fixed((rows, width // 2))],
        [
            jax.ShapeDtypeStruct((rows, width), bf16),
            jax.ShapeDtypeStruct((rows, width // 2), bf16),
        ],
        "attend_back",
        (seg[:, None], seg[None, :], qkv, qkv, qkv, grad_mixed),
        flops=400_000_000_000,
    )


def pack_columns(shard, parts, core):
    n = lax.axis_size("seq")
    rows, width = shard.shape
    part = width // (parts * n)

    def kernel(sc, shard_ref, out):
        for j in range(n):
            for p in range(parts):
                start = (p * n + j) * part
                out[j, :, p * part : (p + 1) * part] = shard_ref[:, start : start + part]

    out = (n, rows, part * parts)
    return grid_call(
        kernel,
        core,
        (1,),
        [fixed(shard.shape)],
        fixed(out),
        jax.ShapeDtypeStruct(out, shard.dtype),
        "pack",
        (shard,),
    )


def join_columns(pieces, parts, halves, core):
    n, rows, width = pieces.shape
    piece = width // (parts * halves)

    def kernel(sc, pieces_ref, out):
        for h in range(halves):
            for j in range(n):
                for p in range(parts):
                    start = (p * n + j) * halves * piece
                    if halves > 1:
                        side = jnp.bitwise_xor(sc[0], h)
                        start = pl.multiple_of(start + side * piece, piece)
                    at = (h * parts + p) * piece
                    value = pieces_ref[j, :, at : at + piece].astype(f32)
                    out[:, pl.ds(start, piece)] = value

    out = (rows, n * width)
    return grid_call(
        kernel,
        core,
        (1,),
        [fixed(pieces.shape)],
        fixed(out),
        jax.ShapeDtypeStruct(out, f32),
        "join_columns",
        (pieces,),
    )


def exchange(pieces):
    return lax.all_to_all(pieces, "seq", 0, 0)


def gather_dp(shard):
    full = lax.all_gather(shard, DP, axis=shard.ndim - 2, tiled=True)
    return full.reshape(-1, full.shape[-1])


def sum_over(value, axes):
    return lax.psum_scatter(value, axes, scatter_dimension=value.ndim - 2, tiled=True)


def to_partner(value):
    return lax.ppermute(value, "core", [(0, 1), (1, 0)])


def column_half(value, index):
    width = value.shape[1] // 2
    return lax.dynamic_slice_in_dim(value, index * width, width, axis=1)


def feed_grads(core, first, first_far, pre, pre_far, act, act_far, ffn, ffn_far):
    n = lax.axis_size("seq")
    chips = lax.axis_size("chip")
    tokens, height = first.shape
    width = ffn_far.shape[1]
    rows = height // (n * chips)

    def kernel(sc, *refs):
        (ao, af, po, pf, go, gf, out) = refs[2 * n :]
        for j in range(n):
            total = dot_tn(refs[j][...], po[...]) + dot_tn(refs[n + j][...], pf[...])
            out[j] = total.astype(bf16)
        total = dot_tn(ao[...], go[...]) + dot_tn(af[...], gf[...])
        out[n:] = total.astype(bf16).reshape(n, rows, width)

    def rows_spec(j):
        return pl.BlockSpec((tokens, rows), lambda o, sc: (0, j * chips + o))

    own_half = pl.BlockSpec((tokens, width), lambda o, sc: (0, sc[0]))
    act_spec = pl.BlockSpec((tokens, n * rows), lambda o, sc: (0, o))
    return grid_call(
        kernel,
        core,
        (chips,),
        [rows_spec(j) for j in range(n)] * 2
        + [act_spec] * 2
        + [own_half, fixed((tokens, width))] * 2,
        pl.BlockSpec((2 * n, rows, width), lambda o, sc: (0, o, 0)),
        jax.ShapeDtypeStruct((2 * n, chips * rows, width), bf16),
        "feed_grads",
        (*[first] * n, *[first_far] * n, act, act_far, pre, pre_far, ffn, ffn_far),
    )


def attn_grad(core, tok, tok_far, mixed, mixed_far, grad_qkv, qkv_far, grad_attn, attn_far):
    n = lax.axis_size("seq")
    chips = lax.axis_size("chip")
    tokens = tok.shape[0]
    half = qkv_far.shape[1] // 3
    out_cols = attn_far.shape[1]
    cols = out_cols // n
    rows = mixed.shape[1] // chips

    def kernel(sc, *refs):
        own_refs, far_refs = refs[:n], refs[n : 2 * n]
        mo, mf, qo, ko, vo, qkv_f, ao, af, out = refs[2 * n :]
        side = (dot_tn(mo[...], ao[...]) + dot_tn(mf[...], af[...])).astype(bf16)
        own = jnp.concatenate([qo[...], ko[...], vo[...]], axis=1)
        for j in range(n):
            total = dot_tn(own_refs[j][...], own) + dot_tn(far_refs[j][...], qkv_f[...])
            out[j, :, : 3 * half] = total.astype(bf16)
            out[j, :, 3 * half :] = side[:, j * cols : (j + 1) * cols]

    def rows_spec(j):
        return pl.BlockSpec((tokens, rows), lambda o, sc: (0, j * chips + o))

    def part_spec(p):
        return pl.BlockSpec((tokens, half), lambda o, sc: (0, 2 * p + sc[0]))

    width = 3 * half + cols
    return grid_call(
        kernel,
        core,
        (chips,),
        [rows_spec(j) for j in range(n)] * 2
        + [rows_spec(0)] * 2
        + [part_spec(p) for p in range(3)]
        + [
            fixed((tokens, 3 * half)),
            pl.BlockSpec((tokens, out_cols), lambda o, sc: (0, sc[0])),
            fixed((tokens, out_cols)),
        ],
        pl.BlockSpec((n, rows, width), lambda o, sc: (0, o, 0)),
        jax.ShapeDtypeStruct((n, chips * rows, width), bf16),
        "attn_grad",
        (
            *[tok] * n,
            *[tok_far] * n,
            mixed,
            mixed_far,
            *[grad_qkv] * 3,
            qkv_far,
            grad_attn,
            attn_far,
        ),
    )


def pick(value, axis, index):
    return lax.dynamic_index_in_dim(value, index, axis, keepdims=False)


def swap_rows(total, split, axis, core):
    value = total.reshape(split)
    return pick(value, axis, core), to_partner(pick(value, axis, 1 - core).astype(bf16))


def join_halves(own, far, core):
    return jnp.where(
        core == 0, jnp.concatenate([own, far], axis=-1), jnp.concatenate([far, own], axis=-1)
    )


def device_count():
    return lax.axis_size("seq") * lax.axis_size("chip") * lax.axis_size("core")


def all_small(vectors):
    count = device_count()
    packed = jnp.concatenate(vectors)
    table = lax.all_to_all(jnp.broadcast_to(packed[None], (count, packed.shape[0])), ALL, 0, 0)
    out = []
    start = 0
    for vector in vectors:
        size = vector.shape[0]
        out.append(table[:, start : start + size].reshape(-1).astype(f32))
        start += size
    return out


def scatter_small(vectors):
    count = device_count()
    packed = jnp.concatenate([v.reshape(count, -1) for v in vectors], axis=1)
    mine = jnp.sum(lax.all_to_all(packed, ALL, 0, 0), axis=0)
    out = []
    start = 0
    for vector in vectors:
        size = vector.shape[0] // count
        out.append(mine[start : start + size])
        start += size
    return out


def gelu_parts(v):
    c = 0.7978845608028654
    t = jnp.tanh(c * (v + 0.044715 * v * v * v))
    value = 0.5 * v * (1.0 + t)
    slope = 0.5 * (1.0 + t) + 0.5 * v * (1.0 - t * t) * c * (1.0 + 3 * 0.044715 * v * v)
    return value, slope


def per_device(
    tokens,
    doc_lengths,
    qkv_weight,
    qv_bias,
    out_weight,
    out_bias,
    norm1_gain,
    norm1_bias,
    in_weight,
    in_bias,
    down_weight,
    down_bias,
    norm2_gain,
    norm2_bias,
    cotangent,
):
    n = lax.axis_size("seq")
    chips = lax.axis_size("chip")
    s = lax.axis_index("seq")
    c = lax.axis_index("core")
    rows = tokens.shape[1]
    width = tokens.shape[2]
    part = width // n
    half = width // 2
    paired = part // chips % 128 == 0
    tok_rows = tokens[0]

    tok_blocks = gather_blocks(tok_rows)
    tok_full = jnp.concatenate(tok_blocks, axis=0)
    out_w = gather_dp(out_weight)
    qkv_moved = exchange(pack_columns(qkv_weight, 3, c))
    vectors = [qv_bias, out_bias, norm1_gain, norm1_bias]
    vectors += [in_bias, down_bias, norm2_gain, norm2_bias]
    small = all_small(after(vectors, qkv_moved))
    qv_full, out_b, gain_one, shift_one, in_b, down_b, gain_two, shift_two = small
    qkv_w = gather_dp(after(qkv_moved, out_w, tok_blocks[1]))
    in_moved = exchange(after(pack_columns(in_weight, 1, c), tok_blocks))
    down_w = gather_dp(after(down_weight, qkv_moved))

    ends = jnp.cumsum(doc_lengths[0])
    steps = jnp.arange(n * rows, dtype=jnp.int32)
    places = jnp.remainder(s - steps // rows, n) * rows + steps % rows
    seg = jnp.sum((places[:, None] >= ends[None, :]).astype(jnp.int32), axis=1)

    q_bias = lax.dynamic_slice_in_dim(qv_full, s * part, part)
    v_bias = lax.dynamic_slice_in_dim(qv_full, width + s * part, part)
    qkv_b = jnp.concatenate([q_bias, jnp.zeros((part,), f32), v_bias])
    qkv = (dot_nn(tok_full, qkv_w) + qkv_b).astype(bf16)
    mixed = attend(qkv, seg, c)
    size = rows // 2
    halves = range(2)
    cut = [slice(h * size, (h + 1) * size) for h in halves]
    attn_partial = dot_nn(mixed, out_w)
    attn_blocks = [send_blocks(split_blocks(attn_partial, h, 2)) for h in halves]
    in_w = gather_dp(after(in_moved, attn_blocks[0], down_w))
    hidden = in_w.shape[1]
    in_bias_own = lax.dynamic_slice_in_dim(in_b, s * hidden, hidden)

    first, normed_one, recip_one, first_blocks = [], [], [], []
    for h in halves:
        if h:
            attn_blocks[h] = after(attn_blocks[h], first[0])
        attn = total_of(attn_blocks[h]) + out_b
        normed, recip = normalize(tok_rows[cut[h]].astype(f32) + attn)
        normed_one.append(normed)
        recip_one.append(recip)
        first.append(normed * gain_one + shift_one)
        first_blocks.append(gather_blocks(first[h].astype(bf16)))

    first_blocks[0] = after(first_blocks[0], first[1])
    act, act_slope, first_full, ffn_blocks, ffn_split = [], [], [], [], []
    for h in halves:
        if h:
            first_blocks[h] = after(first_blocks[h], ffn_split[0])
        first_full.append(jnp.concatenate(first_blocks[h], axis=0))
        act_value, slope = gelu_parts(dot_nn(first_full[h], in_w) + in_bias_own)
        pair = lax.optimization_barrier((act_value.astype(bf16), slope.astype(bf16)))
        act.append(pair[0])
        act_slope.append(pair[1])
        ffn_split.append(split_blocks(dot_nn(act[h], down_w)))
        ffn_blocks.append(send_blocks(ffn_split[h]))

    ffn_blocks[0] = after(ffn_blocks[0], ffn_split[1])
    result, normed_two, grad_h2, grad_ffn, grad_blocks = [], [], [], [], []
    grad_out = cotangent[0].astype(f32)
    for h in halves:
        if h:
            ffn_blocks[h] = after(ffn_blocks[h], grad_ffn[0])
        ffn = total_of(ffn_blocks[h]) + down_b
        normed, recip = normalize(first[h] + ffn)
        normed_two.append(normed)
        result.append((normed * gain_two + shift_two).astype(bf16))
        grad_h2.append(norm_back(grad_out[cut[h]], normed, recip, gain_two))
        grad_ffn.append(grad_h2[h].astype(bf16))
        grad_blocks.append(gather_blocks(grad_ffn[h]))
    result = jnp.concatenate(result, axis=0)
    shift_two_grad = jnp.sum(grad_out, axis=0)
    gain_two_grad = sum(jnp.sum(grad_out[cut[h]] * normed_two[h], axis=0) for h in halves)
    down_b_grad = sum(jnp.sum(grad_ffn[h].astype(f32), axis=0) for h in halves)

    grad_blocks[0] = after(grad_blocks[0], grad_ffn[1])
    grad_ffn_full, grad_pre, back_split, back_blocks = [], [], [], []
    for h in halves:
        if h:
            grad_blocks[h] = after(grad_blocks[h], back_split[0])
        grad_ffn_full.append(jnp.concatenate(grad_blocks[h], axis=0))
        grad_act = dot_nt(grad_ffn_full[h], down_w)
        grad_pre.append((grad_act * act_slope[h].astype(f32)).astype(bf16))
        back_split.append(split_blocks(dot_nt(grad_pre[h], in_w)))
        back_blocks.append(send_blocks(back_split[h]))
    act, first_full, grad_ffn_full, grad_pre = (
        jnp.concatenate(v, axis=0) for v in (act, first_full, grad_ffn_full, grad_pre)
    )
    in_b_grad = jnp.sum(grad_pre.astype(f32), axis=0)
    back_blocks[0] = after(back_blocks[0], back_split[1])
    if paired:
        tok_far, mixed_far, first_far, act_far = (
            to_partner(v) for v in (tok_full, mixed, first_full, act)
        )
        ffn_far = to_partner(column_half(grad_ffn_full, 1 - c))
        pre_far = to_partner(column_half(grad_pre, 1 - c))
        feed = (first_full, first_far, grad_pre, pre_far, act, act_far, grad_ffn_full, ffn_far)
        feed_low = feed_grads(after(c, back_split[1]), *feed)
        back_blocks[1], feed_low = lax.optimization_barrier((back_blocks[1], feed_low))
        feed_sum = sum_over(feed_low, "chip")
    else:
        down_low = dot_tn(act, grad_ffn_full).astype(bf16)
        in_low = dot_tn(first_full, grad_pre).astype(bf16).reshape(n, part, -1)
        down_w_grad = sum_over(down_low, DP).astype(f32)
        in_w_grad = join_columns(exchange(sum_over(in_low, DP)), 1, 1, c)
    grad_first, grad_h1, grad_attn, attn_blocks = [], [], [], []
    for h in halves:
        if h:
            back_blocks[h] = after(back_blocks[h], grad_attn[0])
        grad_first.append(grad_h2[h] + total_of(back_blocks[h]))
        grad_h1.append(norm_back(grad_first[h], normed_one[h], recip_one[h], gain_one))
        grad_attn.append(grad_h1[h].astype(bf16))
        attn_blocks.append(gather_blocks(grad_attn[h]))
    shift_one_grad = sum(jnp.sum(grad_first[h], axis=0) for h in halves)
    gain_one_grad = sum(jnp.sum(grad_first[h] * normed_one[h], axis=0) for h in halves)
    out_b_grad = sum(jnp.sum(grad_attn[h].astype(f32), axis=0) for h in halves)
    grad_h1 = jnp.concatenate(grad_h1, axis=0)
    grad_attn_full = jnp.concatenate([attn_blocks[h][k] for k in range(n) for h in halves], axis=0)
    grad_mixed = dot_nt(grad_attn_full, out_w).astype(bf16)
    grad_qkv, qkv_sent = attend_back(qkv, grad_mixed, seg, c)

    def small_sums(grad_qkv):
        sums = jnp.sum(grad_qkv.astype(f32), axis=0)
        qv_grad = jnp.zeros((2 * width,), f32)
        qv_grad = lax.dynamic_update_slice_in_dim(qv_grad, sums[:part], s * part, 0)
        qv_grad = lax.dynamic_update_slice_in_dim(qv_grad, sums[2 * part :], width + s * part, 0)
        in_b_all = jnp.zeros((n * hidden,), f32)
        in_b_all = lax.dynamic_update_slice_in_dim(in_b_all, in_b_grad, s * hidden, 0)
        return scatter_small(
            [
                qv_grad,
                out_b_grad,
                gain_one_grad,
                shift_one_grad,
                in_b_all,
                down_b_grad,
                gain_two_grad,
                shift_two_grad,
            ]
        )

    if paired:
        attn_far = to_partner(column_half(grad_attn_full, 1 - c))
        args = (tok_full, tok_far, mixed, mixed_far)
        qkv_far = to_partner(qkv_sent)
        attn_low = attn_grad(c, *args, grad_qkv, qkv_far, grad_attn_full, attn_far)
        attn_sum = sum_over(attn_low, "chip")
        last_split = split_blocks(dot_nt(after(grad_qkv, attn_low), qkv_w))
        last_blocks = send_blocks(last_split)
        small_grads = small_sums(after(grad_qkv, last_blocks[1]))
        last_blocks[-1] = after(last_blocks[-1], small_grads)
        feed_sum = after(feed_sum, last_blocks)
        in_own, in_far = swap_rows(feed_sum[:n], (n, 2, -1, half), 1, c)
        in_pieces = exchange(jnp.concatenate([in_own, in_far], axis=2))
        in_w_grad = join_columns(in_pieces, 1, 2, c)
        down_own, down_far = swap_rows(feed_sum[n:], (2, -1, half), 0, c)
        down_w_grad = join_halves(down_own.astype(f32), down_far.astype(f32), c)
        attn_sum = after(attn_sum, in_far, down_own)
        attn_own, attn_far = swap_rows(attn_sum, (n, 2, -1, half), 1, c)
        split = 3 * part // 2
        pieces = jnp.concatenate([attn_own[:, :, :split], attn_far[:, :, :split]], 2)
        qkv_w_grad = join_columns(exchange(pieces), 3, 2, c)
        out_own, out_far = (
            jnp.concatenate([v[j, :, split:] for j in range(n)], axis=1).astype(f32)
            for v in (attn_own, attn_far)
        )
        out_w_grad = join_halves(out_own, out_far, c)
    else:
        last_split = split_blocks(dot_nt(grad_qkv, qkv_w))
        last_blocks = send_blocks(last_split)
        small_grads = small_sums(after(grad_qkv, last_split))
        attn_low = after(dot_tn(tok_full, grad_qkv).astype(bf16), last_split)
        out_w_grad = sum_over(dot_tn(mixed, grad_attn_full).astype(bf16), DP).astype(f32)
        pieces = exchange(sum_over(attn_low.reshape(n, part, -1), DP))
        qkv_w_grad = join_columns(pieces, 3, 1, c)
    last_blocks = after(last_blocks, small_grads)
    input_grad = (grad_h1 + total_of(last_blocks)).astype(bf16)
    return (
        result[None],
        input_grad[None],
        qkv_w_grad,
        small_grads[0],
        out_w_grad,
        small_grads[1],
        small_grads[2],
        small_grads[3],
        in_w_grad,
        small_grads[4],
        down_w_grad,
        small_grads[5],
        small_grads[6],
        small_grads[7],
    )


def solution(mesh):
    devices = mesh.devices
    split = jax.sharding.Mesh(devices.reshape(devices.shape[0], -1, 2), ALL)
    rows = P(ALL, None)
    flat = P(ALL)
    tok = P(DP, "seq", None)
    ins = (tok, P(DP, None), rows, flat, rows, *[flat] * 3, rows, flat, rows, *[flat] * 3, tok)
    outs = (tok, tok, rows, flat, rows, *[flat] * 3, rows, flat, rows, *[flat] * 3)
    return jax.shard_map(per_device, mesh=split, in_specs=ins, out_specs=outs, check_vma=False)
```

```python
import jax
import jax.numpy as jnp
from jax import lax
from jax.experimental import pallas as pl
from jax.experimental.pallas import tpu as pltpu
from jax.sharding import PartitionSpec as P

HEAD_DIM = 128
eps_norm = 1e-06
f32 = jnp.float32
bf16 = jnp.bfloat16
DP = ("chip", "core")
ALL = ("seq", "chip", "core")


def after(value, *others):
    return lax.optimization_barrier((value, *others))[0]


def shift(value, step):
    n = lax.axis_size("seq")
    return lax.ppermute(value, "seq", [(i, (i + step) % n) for i in range(n)])


def gather_blocks(rows):
    n = lax.axis_size("seq")
    return [rows] + [shift(rows, k) for k in range(1, n)]


def send_blocks(blocks):
    return [blocks[0]] + [shift(blocks[k], -k) for k in range(1, len(blocks))]


def total_of(blocks):
    total = blocks[0]
    for block in blocks[1:]:
        total = total + block.astype(f32)
    return total


def normalize(hidden):
    center = hidden - jnp.mean(hidden, axis=-1, keepdims=True)
    spread = jnp.mean(center * center, axis=-1, keepdims=True)
    recip = lax.rsqrt(spread + eps_norm)
    return (center * recip, recip)


def norm_back(grad_out, normed, recip, gain):
    scaled = grad_out * gain
    return recip * (
        scaled
        - jnp.mean(scaled, axis=-1, keepdims=True)
        - normed * jnp.mean(scaled * normed, axis=-1, keepdims=True)
    )


def dot_nn(a, b):
    return lax.dot_general(a, b, (((1,), (0,)), ((), ())), preferred_element_type=f32)


def dot_nt(a, b):
    return lax.dot_general(a, b, (((1,), (1,)), ((), ())), preferred_element_type=f32)


def dot_tn(a, b):
    return lax.dot_general(a, b, (((0,), (0,)), ((), ())), preferred_element_type=f32)


def grid_call(kernel, scalar, grid, in_specs, out_specs, out_shape, name, args, cost=None):
    grid_spec = pltpu.PrefetchScalarGridSpec(
        num_scalar_prefetch=1, grid=grid, in_specs=in_specs, out_specs=out_specs
    )
    return pl.pallas_call(
        kernel,
        grid_spec=grid_spec,
        out_shape=out_shape,
        compiler_params=pltpu.CompilerParams(vmem_limit_bytes=56 << 20),
        cost_estimate=cost
        and pl.CostEstimate(flops=cost[0], transcendentals=0, bytes_accessed=cost[1]),
        name=name,
    )(jnp.reshape(scalar, (1,)).astype(jnp.int32), *args)


def fixed(shape):
    return pl.BlockSpec(shape, lambda g, sc: (0,) * len(shape))


def tile_of(width, most):
    return next(t for t in range(most, 0, -128) if width % t == 0)


def product(
    core, blocks, w, finish, outs, name, nt=False, extra=(), more=(), keep=False, send=False, at=None,
    most=1024,
):
    depth = blocks[0].shape[1]
    sizes = [at[0]] if at else [block.shape[0] for block in blocks]
    rows = sum(sizes)
    width = w.shape[0] if nt else w.shape[1]
    tile = tile_of(width, most)
    count = len(blocks)

    def kernel(sc, *refs):
        block_refs, w_ref = refs[:count], refs[count]
        extra_refs = refs[count + 1 : count + 1 + len(extra)]
        out_refs = refs[count + 1 + len(extra) :]
        step = pl.program_id(0)
        if keep:
            full_ref = out_refs[-1]

            @pl.when(step == 0)
            def _():
                start = 0
                for ref, size in zip(block_refs, sizes):
                    full_ref[start : start + size] = ref[...]
                    start += size
                if send:
                    side = pl.multiple_of((1 - sc[0]) * (depth // 2), 128)
                    out_refs[-2][:rows] = full_ref[:rows, pl.ds(side, depth // 2)]

            value = full_ref[:rows]
        else:
            value = block_refs[0][...]
        dot = dot_nt if nt else dot_nn
        finish(dot(value, w_ref[...]), extra_refs, out_refs, step, sc[0])

    w_spec = (
        pl.BlockSpec((tile, depth), lambda i, sc: (i, 0))
        if nt
        else pl.BlockSpec((depth, tile), lambda i, sc: (0, i))
    )
    tiled = lambda size: pl.BlockSpec((size, tile), lambda i, sc: (0, i))
    index = at[1] if at else 0
    return grid_call(
        kernel,
        core,
        (width // tile,),
        [pl.BlockSpec((size, depth), lambda i, sc: (index, 0)) for size in sizes]
        + [w_spec]
        + [tiled(array.shape[0]) for array in extra],
        [tiled(size) for size, _ in outs] + [fixed(shape) for shape in more],
        [jax.ShapeDtypeStruct((size, width), kind) for size, kind in outs]
        + [jax.ShapeDtypeStruct(shape, bf16) for shape in more],
        name,
        (*blocks, w, *extra),
        cost=(2 * rows * depth * width, 2 * (rows * depth + width * depth + rows * width)),
    )


def split_product(core, value, w, name, nt=False, parts=1, at=None):
    n = lax.axis_size("seq")
    size = (at[0] if at else value.shape[0]) // (n * parts)

    def finish(total, extra, outs, step, core):
        for p in range(parts):
            for k in range(n):
                start = (k * parts + p) * size
                ref = outs[p * n + k]
                ref[...] = total[start : start + size].astype(ref.dtype)

    outs = [(size, f32 if k == 0 else bf16) for p in range(parts) for k in range(n)]
    got = product(core, [value], w, finish, outs, name, nt=nt, at=at)
    return [list(got[p * n : (p + 1) * n]) for p in range(parts)]


def softmax_of(q, k, seg_col, seg_row):
    scores = dot_nt(q, k) * HEAD_DIM ** (-0.5)
    scores = jnp.where(seg_col == seg_row, scores, -1e30)
    terms = jnp.exp(scores - jnp.max(scores, axis=1, keepdims=True))
    return terms / jnp.sum(terms, axis=1, keepdims=True)


def attend_kernel(core, seg_col, seg_row, q, k, v, mixed):
    probs = softmax_of(q[...], k[...], seg_col[...], seg_row[...])
    mixed[...] = dot_nn(probs.astype(bf16), v[...]).astype(bf16)


def attend_back_kernel(core, seg_col, seg_row, q, k, v, gm, grad, sent):
    heads = pl.num_programs(0)
    head = pl.program_id(0)
    probs = softmax_of(q[...], k[...], seg_col[...], seg_row[...])
    grad_probs = dot_nt(gm[...], v[...])
    products = jnp.sum(probs * grad_probs, axis=1, keepdims=True)
    grad_scores = (probs * (grad_probs - products)).astype(bf16)
    scale = HEAD_DIM ** (-0.5)
    half = heads // 2

    def put(part, value):
        value = value.astype(bf16)
        start = pl.multiple_of((part * heads + head) * HEAD_DIM, HEAD_DIM)
        grad[:, pl.ds(start, HEAD_DIM)] = value

        @pl.when(head // half != core[0])
        def _():
            into = pl.multiple_of((part * half + head % half) * HEAD_DIM, HEAD_DIM)
            sent[:, pl.ds(into, HEAD_DIM)] = value

    put(0, dot_nn(grad_scores, k[...]) * scale)
    put(1, dot_tn(grad_scores, q[...]) * scale)
    put(2, dot_tn(probs.astype(bf16), gm[...]))


def head_spec(rows, offset):
    return pl.BlockSpec((rows, HEAD_DIM), lambda h, sc: (0, offset + h))


def qkv_specs(rows, heads):
    return [
        fixed((rows, 1)),
        fixed((1, rows)),
        head_spec(rows, 0),
        head_spec(rows, heads),
        head_spec(rows, 2 * heads),
    ]


def attend(qkv, seg, core):
    rows, width = qkv.shape
    heads = width // (3 * HEAD_DIM)
    return grid_call(
        attend_kernel,
        core,
        (heads,),
        qkv_specs(rows, heads),
        head_spec(rows, 0),
        jax.ShapeDtypeStruct((rows, width // 3), bf16),
        "attend",
        (seg[:, None], seg[None, :], qkv, qkv, qkv),
    )


def attend_back(qkv, grad_mixed, seg, core):
    rows, width = qkv.shape
    heads = width // (3 * HEAD_DIM)
    return grid_call(
        attend_back_kernel,
        core,
        (heads,),
        qkv_specs(rows, heads) + [head_spec(rows, 0)],
        [fixed((rows, width)), fixed((rows, width // 2))],
        [
            jax.ShapeDtypeStruct((rows, width), bf16),
            jax.ShapeDtypeStruct((rows, width // 2), bf16),
        ],
        "attend_back",
        (seg[:, None], seg[None, :], qkv, qkv, qkv, grad_mixed),
        cost=(400_000_000_000, 1),
    )


def pack_columns(shard, parts, core):
    n = lax.axis_size("seq")
    rows, width = shard.shape
    part = width // (parts * n)

    def kernel(sc, shard_ref, out):
        for j in range(n):
            for p in range(parts):
                start = (p * n + j) * part
                out[j, :, p * part : (p + 1) * part] = shard_ref[:, start : start + part]

    out = (n, rows, part * parts)
    return grid_call(
        kernel,
        core,
        (1,),
        [fixed(shard.shape)],
        fixed(out),
        jax.ShapeDtypeStruct(out, shard.dtype),
        "pack",
        (shard,),
    )


def join_columns(pieces, parts, halves, core):
    n, rows, width = pieces.shape
    piece = width // (parts * halves)

    def kernel(sc, pieces_ref, out):
        for h in range(halves):
            for j in range(n):
                for p in range(parts):
                    start = (p * n + j) * halves * piece
                    if halves > 1:
                        side = jnp.bitwise_xor(sc[0], h)
                        start = pl.multiple_of(start + side * piece, piece)
                    at = (h * parts + p) * piece
                    value = pieces_ref[j, :, at : at + piece].astype(f32)
                    out[:, pl.ds(start, piece)] = value

    out = (rows, n * width)
    return grid_call(
        kernel,
        core,
        (1,),
        [fixed(pieces.shape)],
        fixed(out),
        jax.ShapeDtypeStruct(out, f32),
        "join_columns",
        (pieces,),
    )


def exchange(pieces):
    return lax.all_to_all(pieces, "seq", 0, 0)


def gather_dp(shard):
    full = lax.all_gather(shard, DP, axis=shard.ndim - 2, tiled=True)
    return full.reshape(-1, full.shape[-1])


def sum_over(value, axes):
    return lax.psum_scatter(value, axes, scatter_dimension=value.ndim - 2, tiled=True)


def to_partner(value):
    return lax.ppermute(value, "core", [(0, 1), (1, 0)])


def feed_grads(core, pairs, pre, ffn, far):
    n = lax.axis_size("seq")
    chips = lax.axis_size("chip")
    tokens = pre[0].shape[0]
    height = pairs[0].shape[1]
    width = far[0].shape[1]
    rows = height // (n * chips)
    parts = len(pairs)

    def kernel(sc, *refs):
        act_refs = refs[n * parts : (n + 1) * parts]
        pre_refs = refs[(n + 1) * parts : (n + 2) * parts]
        ffn_refs = refs[(n + 2) * parts : (n + 3) * parts]
        out = refs[-1]
        for j in range(n):
            joined = zip(refs[j * parts : (j + 1) * parts], pre_refs)
            out[j] = sum(dot_tn(a[...], b[...]) for a, b in joined).astype(bf16)
        total = sum(dot_tn(a[...], b[...]) for a, b in zip(act_refs, ffn_refs))
        out[n:] = total.astype(bf16).reshape(n, rows, width)

    def rows_spec(j):
        return pl.BlockSpec((tokens, rows), lambda o, sc: (0, j * chips + o))

    own_half = [pl.BlockSpec((tokens, width), lambda o, sc: (0, sc[0]))] * len(pre)
    far_top = [pl.BlockSpec((tokens, width), lambda o, sc: (0, 0))] * len(far)
    far_low = [pl.BlockSpec((tokens, width), lambda o, sc: (1, 0))] * len(far)
    act_spec = pl.BlockSpec((tokens, n * rows), lambda o, sc: (1, o))
    return grid_call(
        kernel,
        core,
        (chips,),
        [rows_spec(j) for j in range(n) for _ in range(parts)]
        + [act_spec] * parts
        + own_half
        + far_low
        + own_half
        + far_top,
        pl.BlockSpec((2 * n, rows, width), lambda o, sc: (0, o, 0)),
        jax.ShapeDtypeStruct((2 * n, chips * rows, width), bf16),
        "feed_grads",
        (*[pair for _ in range(n) for pair in pairs], *pairs, *pre, *far, *ffn, *far),
    )


def attn_grad(core, tok, tok_far, mixed, mixed_far, grad_qkv, qkv_far, grad_attn, attn_far):
    n = lax.axis_size("seq")
    chips = lax.axis_size("chip")
    tokens = tok.shape[0]
    half = qkv_far.shape[1] // 3
    out_cols = attn_far.shape[1]
    cols = out_cols // n
    rows = mixed.shape[1] // chips * 2
    steps = chips // 2

    def kernel(sc, *refs):
        own_refs, far_refs = refs[:n], refs[n : 2 * n]
        mo, mf, qo, ko, vo, qkv_f, ao, af, out = refs[2 * n :]
        side = (dot_tn(mo[...], ao[...]) + dot_tn(mf[...], af[...])).astype(bf16)
        own = jnp.concatenate([qo[...], ko[...], vo[...]], axis=1)
        for j in range(n):
            total = dot_tn(own_refs[j][...], own) + dot_tn(far_refs[j][...], qkv_f[...])
            out[j, :, : 3 * half] = total.astype(bf16)
            out[j, :, 3 * half :] = side[:, j * cols : (j + 1) * cols]

    def rows_spec(j):
        return pl.BlockSpec((tokens, rows), lambda o, sc: (0, j * steps + o))

    def part_spec(p):
        return pl.BlockSpec((tokens, half), lambda o, sc: (0, 2 * p + sc[0]))

    width = 3 * half + cols
    return grid_call(
        kernel,
        core,
        (steps,),
        [rows_spec(j) for j in range(n)] * 2
        + [rows_spec(0)] * 2
        + [part_spec(p) for p in range(3)]
        + [
            fixed((tokens, 3 * half)),
            pl.BlockSpec((tokens, out_cols), lambda o, sc: (0, sc[0])),
            fixed((tokens, out_cols)),
        ],
        pl.BlockSpec((n, rows, width), lambda o, sc: (0, o, 0)),
        jax.ShapeDtypeStruct((n, steps * rows, width), bf16),
        "attn_grad",
        (
            *[tok] * n,
            *[tok_far] * n,
            mixed,
            mixed_far,
            *[grad_qkv] * 3,
            qkv_far,
            grad_attn,
            attn_far,
        ),
    )


def pick(value, axis, index):
    return lax.dynamic_index_in_dim(value, index, axis, keepdims=False)


def swap_rows(total, split, axis, core):
    value = total.reshape(split)
    return pick(value, axis, core), to_partner(pick(value, axis, 1 - core).astype(bf16))


def join_halves(own, far, core):
    return jnp.where(
        core == 0, jnp.concatenate([own, far], axis=-1), jnp.concatenate([far, own], axis=-1)
    )


def device_count():
    return lax.axis_size("seq") * lax.axis_size("chip") * lax.axis_size("core")


def all_small(vectors):
    count = device_count()
    packed = jnp.concatenate(vectors)
    table = lax.all_to_all(jnp.broadcast_to(packed[None], (count, packed.shape[0])), ALL, 0, 0)
    out = []
    start = 0
    for vector in vectors:
        size = vector.shape[0]
        out.append(table[:, start : start + size].reshape(-1).astype(f32))
        start += size
    return out


def scatter_small(vectors):
    count = device_count()
    packed = jnp.concatenate([v.reshape(count, -1) for v in vectors], axis=1)
    mine = jnp.sum(lax.all_to_all(packed, ALL, 0, 0), axis=0)
    out = []
    start = 0
    for vector in vectors:
        size = vector.shape[0] // count
        out.append(mine[start : start + size])
        start += size
    return out


def gelu_parts(v):
    c = 0.7978845608028654
    t = jnp.tanh(c * (v + 0.044715 * v * v * v))
    value = 0.5 * v * (1.0 + t)
    slope = 0.5 * (1.0 + t) + 0.5 * v * (1.0 - t * t) * c * (1.0 + 3 * 0.044715 * v * v)
    return value, slope


def per_device(
    tokens,
    doc_lengths,
    qkv_weight,
    qv_bias,
    out_weight,
    out_bias,
    norm1_gain,
    norm1_bias,
    in_weight,
    in_bias,
    down_weight,
    down_bias,
    norm2_gain,
    norm2_bias,
    cotangent,
):
    n = lax.axis_size("seq")
    chips = lax.axis_size("chip")
    s = lax.axis_index("seq")
    c = lax.axis_index("core")
    rows = tokens.shape[1]
    width = tokens.shape[2]
    part = width // n
    half = width // 2
    paired = part // chips % 128 == 0 and in_weight.shape[1] == n * width
    tok_rows = tokens[0]

    tok_blocks = gather_blocks(tok_rows)
    out_w = gather_dp(out_weight)
    qkv_moved = exchange(pack_columns(qkv_weight, 3, c))
    vectors = [qv_bias, out_bias, norm1_gain, norm1_bias]
    vectors += [in_bias, down_bias, norm2_gain, norm2_bias]
    small = all_small(after(vectors, qkv_moved))
    qv_full, out_b, gain_one, shift_one, in_b, down_b, gain_two, shift_two = small
    qkv_w = gather_dp(after(qkv_moved, out_w, tok_blocks[1]))
    in_moved = exchange(after(pack_columns(in_weight, 1, c), tok_blocks))
    down_w = gather_dp(after(down_weight, qkv_moved))

    ends = jnp.cumsum(doc_lengths[0])
    steps = jnp.arange(n * rows, dtype=jnp.int32)
    places = jnp.remainder(s - steps // rows, n) * rows + steps % rows
    seg = jnp.sum((places[:, None] >= ends[None, :]).astype(jnp.int32), axis=1)

    q_bias = lax.dynamic_slice_in_dim(qv_full, s * part, part)
    v_bias = lax.dynamic_slice_in_dim(qv_full, width + s * part, part)
    qkv_b = jnp.concatenate([q_bias, jnp.zeros((part,), f32), v_bias])

    def finish_qkv(total, extra, outs, step, core):
        outs[0][...] = (total + extra[0][...]).astype(bf16)

    total_rows = n * rows
    qkv, tok_full = product(
        c,
        tok_blocks,
        qkv_w,
        finish_qkv,
        [(total_rows, bf16)],
        "qkv",
        extra=(qkv_b[None],),
        more=[(total_rows, width)],
        keep=True,
    )
    mixed = attend(qkv, seg, c)
    size = rows // 2
    halves = range(2)
    cut = [slice(h * size, (h + 1) * size) for h in halves]
    attn_split = split_product(c, mixed, out_w, "out", parts=2)
    attn_blocks = [send_blocks(blocks) for blocks in attn_split]
    in_w = gather_dp(after(in_moved, attn_blocks[0]))
    hidden = in_w.shape[1]
    in_bias_own = lax.dynamic_slice_in_dim(in_b, s * hidden, hidden)

    first, normed_one, recip_one, first_blocks = [], [], [], []
    for h in halves:
        if h:
            attn_blocks[h] = after(attn_blocks[h], first[0], down_w)
        attn = total_of(attn_blocks[h]) + out_b
        normed, recip = normalize(tok_rows[cut[h]].astype(f32) + attn)
        normed_one.append(normed)
        recip_one.append(recip)
        first.append(normed * gain_one + shift_one)
        first_blocks.append(gather_blocks(first[h].astype(bf16)))

    first_blocks[0] = after(first_blocks[0], first[1])

    def finish_in(total, extra, outs, step, core):
        value, slope = gelu_parts(total + extra[0][...])
        outs[0][...] = slope.astype(bf16)
        tile = value.shape[1]
        start = pl.multiple_of(step * tile, tile)
        outs[1][:, pl.ds(start, tile)] = value.astype(bf16)

    def finish_pair(total, extra, outs, step, core):
        value, slope = gelu_parts(total + extra[0][...])
        outs[0][...] = slope.astype(bf16)
        tile = value.shape[1]
        start = pl.multiple_of(step * tile, tile)
        outs[1][rows_half:, pl.ds(start, tile)] = value.astype(bf16)

    rows_half = n * size
    act_slope, pairs, ffn_blocks, ffn_split = [], [], [], []
    for h in halves:
        if h:
            first_blocks[h] = after(first_blocks[h], ffn_split[0])
        args = (c, first_blocks[h], in_w)
        outs = [(rows_half, bf16)]
        bias = (in_bias_own[None],)
        if paired:
            more = [(2 * rows_half, width)]
            slope, pair = product(
                *args, finish_pair, outs, "in", extra=bias, more=more, keep=True, most=512
            )
            ffn_split += split_product(c, pair, down_w, "down", at=(rows_half, 1))
        else:
            more = [(rows_half, hidden), (rows_half, width)]
            slope, *pair = product(*args, finish_in, outs, "in", extra=bias, more=more, keep=True)
            ffn_split += split_product(c, pair[0], down_w, "down")
        act_slope.append(slope)
        pairs.append(pair)
        ffn_blocks.append(send_blocks(ffn_split[h]))

    ffn_blocks[0] = after(ffn_blocks[0], ffn_split[1])
    result, normed_two, grad_h2, grad_ffn, grad_blocks = [], [], [], [], []
    grad_out = cotangent[0].astype(f32)
    for h in halves:
        if h:
            ffn_blocks[h] = after(ffn_blocks[h], grad_ffn[0])
        ffn = total_of(ffn_blocks[h]) + down_b
        normed, recip = normalize(first[h] + ffn)
        normed_two.append(normed)
        result.append((normed * gain_two + shift_two).astype(bf16))
        grad_h2.append(norm_back(grad_out[cut[h]], normed, recip, gain_two))
        grad_ffn.append(grad_h2[h].astype(bf16))
        grad_blocks.append(gather_blocks(grad_ffn[h]))
    result = jnp.concatenate(result, axis=0)
    shift_two_grad = jnp.sum(grad_out, axis=0)
    gain_two_grad = sum(jnp.sum(grad_out[cut[h]] * normed_two[h], axis=0) for h in halves)
    down_b_grad = sum(jnp.sum(grad_ffn[h].astype(f32), axis=0) for h in halves)

    grad_blocks[0] = after(grad_blocks[0], grad_ffn[1])
    if paired:
        pairs_far = [to_partner(v) for v in pairs]
        grad_blocks = [after(grad_blocks[0], pairs_far), grad_blocks[1]]

    def finish_pre(total, extra, outs, step, core):
        value = (total * extra[0][...].astype(f32)).astype(bf16)
        outs[0][...] = value
        if paired:
            tile = value.shape[1]
            steps = hidden // (2 * tile)

            @pl.when(step // steps != core)
            def _():
                start = pl.multiple_of(step % steps * tile, tile)
                outs[1][rows_half:, pl.ds(start, tile)] = value

    grad_ffn_full, grad_pre, grad_sent, back_split, back_blocks = [], [], [], [], []
    for h in halves:
        if h:
            grad_blocks[h] = after(grad_blocks[h], back_split[0])
        sent = [(2 * rows_half, half)] if paired else []
        got = product(
            c,
            grad_blocks[h],
            down_w,
            finish_pre,
            [(rows_half, bf16)],
            "pre_grad",
            nt=True,
            extra=(act_slope[h],),
            more=sent + [(rows_half, width)],
            keep=True,
            send=paired,
        )
        grad_pre.append(got[0])
        grad_sent.append(got[1])
        grad_ffn_full.append(got[-1])
        back_split += split_product(c, grad_pre[h], in_w, "back", nt=True)
        back_blocks.append(send_blocks(back_split[h]))
    in_b_grad = sum(jnp.sum(v.astype(f32), axis=0) for v in grad_pre)
    back_blocks[0] = after(back_blocks[0], back_split[1])
    if paired:
        tok_far, mixed_far = to_partner(tok_full), to_partner(mixed)
        grad_far = [to_partner(v) for v in grad_sent]
        feed = (pairs + pairs_far, grad_pre, grad_ffn_full, grad_far)
        feed_low = feed_grads(after(c, back_split[1]), *feed)
        back_blocks[1], feed_low = lax.optimization_barrier((back_blocks[1], feed_low))
        feed_sum = sum_over(feed_low, "chip")
    else:
        act, first_full = (jnp.concatenate([p[i] for p in pairs], axis=0) for i in range(2))
        grad_ffn_full, grad_pre = (jnp.concatenate(v, axis=0) for v in (grad_ffn_full, grad_pre))
        down_low = dot_tn(act, grad_ffn_full).astype(bf16)
        in_low = dot_tn(first_full, grad_pre).astype(bf16).reshape(n, part, -1)
        down_w_grad = sum_over(down_low, DP).astype(f32)
        in_w_grad = join_columns(exchange(sum_over(in_low, DP)), 1, 1, c)
    grad_first, grad_h1, grad_attn, attn_blocks = [], [], [], []
    for h in halves:
        if h:
            back_blocks[h] = after(back_blocks[h], grad_attn[0])
        grad_first.append(grad_h2[h] + total_of(back_blocks[h]))
        grad_h1.append(norm_back(grad_first[h], normed_one[h], recip_one[h], gain_one))
        grad_attn.append(grad_h1[h].astype(bf16))
        attn_blocks.append(gather_blocks(grad_attn[h]))
    shift_one_grad = sum(jnp.sum(grad_first[h], axis=0) for h in halves)
    gain_one_grad = sum(jnp.sum(grad_first[h] * normed_one[h], axis=0) for h in halves)
    out_b_grad = sum(jnp.sum(grad_attn[h].astype(f32), axis=0) for h in halves)
    grad_h1 = jnp.concatenate(grad_h1, axis=0)

    def finish_mixed(total, extra, outs, step, core):
        outs[0][...] = total.astype(bf16)

    blocks = [attn_blocks[h][k] for k in range(n) for h in halves]
    grad_mixed, attn_sent, grad_attn_full = product(
        c,
        blocks,
        out_w,
        finish_mixed,
        [(total_rows, bf16)],
        "mixed_grad",
        nt=True,
        more=[(total_rows, half), (total_rows, width)],
        keep=True,
        send=True,
    )
    grad_qkv, qkv_sent = attend_back(qkv, grad_mixed, seg, c)

    def small_sums(grad_qkv):
        sums = jnp.sum(grad_qkv.astype(f32), axis=0)
        qv_grad = jnp.zeros((2 * width,), f32)
        qv_grad = lax.dynamic_update_slice_in_dim(qv_grad, sums[:part], s * part, 0)
        qv_grad = lax.dynamic_update_slice_in_dim(qv_grad, sums[2 * part :], width + s * part, 0)
        in_b_all = jnp.zeros((n * hidden,), f32)
        in_b_all = lax.dynamic_update_slice_in_dim(in_b_all, in_b_grad, s * hidden, 0)
        return scatter_small(
            [
                qv_grad,
                out_b_grad,
                gain_one_grad,
                shift_one_grad,
                in_b_all,
                down_b_grad,
                gain_two_grad,
                shift_two_grad,
            ]
        )

    if paired:
        attn_far = to_partner(attn_sent)
        args = (tok_full, tok_far, mixed, mixed_far)
        qkv_far = to_partner(qkv_sent)
        attn_low = attn_grad(c, *args, grad_qkv, qkv_far, grad_attn_full, attn_far)
        attn_sum = sum_over(attn_low, "chip")
        last_split = split_product(c, after(grad_qkv, attn_low), qkv_w, "last", nt=True)[0]
        last_blocks = send_blocks(last_split)
        small_grads = small_sums(after(grad_qkv, last_blocks[1]))
        last_blocks[-1] = after(last_blocks[-1], small_grads)
        feed_sum = after(feed_sum, last_blocks)
        in_own, in_far = swap_rows(feed_sum[:n], (n, 2, -1, half), 1, c)
        in_pieces = exchange(jnp.concatenate([in_own, in_far], axis=2))
        in_w_grad = join_columns(in_pieces, 1, 2, c)
        down_own, down_far = swap_rows(feed_sum[n:], (2, -1, half), 0, c)
        down_w_grad = join_halves(down_own.astype(f32), down_far.astype(f32), c)
        attn_sum = after(attn_sum, in_far, down_own)
        attn_own, attn_far = swap_rows(attn_sum, (n, 2, -1, half), 1, c)
        split = 3 * part // 2
        pieces = jnp.concatenate([attn_own[:, :, :split], attn_far[:, :, :split]], 2)
        qkv_w_grad = join_columns(exchange(pieces), 3, 2, c)
        out_own, out_far = (
            jnp.concatenate([v[j, :, split:] for j in range(n)], axis=1).astype(f32)
            for v in (attn_own, attn_far)
        )
        out_w_grad = join_halves(out_own, out_far, c)
    else:
        last_split = split_product(c, grad_qkv, qkv_w, "last", nt=True)[0]
        last_blocks = send_blocks(last_split)
        small_grads = small_sums(after(grad_qkv, last_split))
        attn_low = after(dot_tn(tok_full, grad_qkv).astype(bf16), last_split)
        out_w_grad = sum_over(dot_tn(mixed, grad_attn_full).astype(bf16), DP).astype(f32)
        pieces = exchange(sum_over(attn_low.reshape(n, part, -1), DP))
        qkv_w_grad = join_columns(pieces, 3, 1, c)
    last_blocks = after(last_blocks, small_grads)
    input_grad = (grad_h1 + total_of(last_blocks)).astype(bf16)
    return (
        result[None],
        input_grad[None],
        qkv_w_grad,
        small_grads[0],
        out_w_grad,
        small_grads[1],
        small_grads[2],
        small_grads[3],
        in_w_grad,
        small_grads[4],
        down_w_grad,
        small_grads[5],
        small_grads[6],
        small_grads[7],
    )


def solution(mesh):
    devices = mesh.devices
    split = jax.sharding.Mesh(devices.reshape(devices.shape[0], -1, 2), ALL)
    rows = P(ALL, None)
    flat = P(ALL)
    tok = P(DP, "seq", None)
    ins = (tok, P(DP, None), rows, flat, rows, *[flat] * 3, rows, flat, rows, *[flat] * 3, tok)
    outs = (tok, tok, rows, flat, rows, *[flat] * 3, rows, flat, rows, *[flat] * 3)
    return jax.shard_map(per_device, mesh=split, in_specs=ins, out_specs=outs, check_vma=False)
```

```python
import jax
import jax.numpy as jnp
from jax import lax
from jax.experimental import pallas as pl
from jax.experimental.pallas import tpu as pltpu
from jax.sharding import PartitionSpec as P

HEAD_DIM = 128
eps_norm = 1e-06
f32 = jnp.float32
bf16 = jnp.bfloat16
DP = ("chip", "core")
ALL = ("seq", "chip", "core")


def after(value, *others):
    return lax.optimization_barrier((value, *others))[0]


def shift(value, step):
    n = lax.axis_size("seq")
    return lax.ppermute(value, "seq", [(i, (i + step) % n) for i in range(n)])


def gather_blocks(rows):
    n = lax.axis_size("seq")
    return [rows] + [shift(rows, k) for k in range(1, n)]


def send_blocks(blocks):
    return [blocks[0]] + [shift(blocks[k], -k) for k in range(1, len(blocks))]


def total_of(blocks):
    total = blocks[0]
    for block in blocks[1:]:
        total = total + block.astype(f32)
    return total


def normalize(hidden):
    center = hidden - jnp.mean(hidden, axis=-1, keepdims=True)
    spread = jnp.mean(center * center, axis=-1, keepdims=True)
    recip = lax.rsqrt(spread + eps_norm)
    return (center * recip, recip)


def norm_back(grad_out, normed, recip, gain):
    scaled = grad_out * gain
    return recip * (
        scaled
        - jnp.mean(scaled, axis=-1, keepdims=True)
        - normed * jnp.mean(scaled * normed, axis=-1, keepdims=True)
    )


def dot_nn(a, b):
    return lax.dot_general(a, b, (((1,), (0,)), ((), ())), preferred_element_type=f32)


def dot_nt(a, b):
    return lax.dot_general(a, b, (((1,), (1,)), ((), ())), preferred_element_type=f32)


def dot_tn(a, b):
    return lax.dot_general(a, b, (((0,), (0,)), ((), ())), preferred_element_type=f32)


def grid_call(kernel, scalar, grid, in_specs, out_specs, out_shape, name, args, cost=None):
    grid_spec = pltpu.PrefetchScalarGridSpec(
        num_scalar_prefetch=1, grid=grid, in_specs=in_specs, out_specs=out_specs
    )
    return pl.pallas_call(
        kernel,
        grid_spec=grid_spec,
        out_shape=out_shape,
        compiler_params=pltpu.CompilerParams(vmem_limit_bytes=56 << 20),
        cost_estimate=cost
        and pl.CostEstimate(flops=cost[0], transcendentals=0, bytes_accessed=cost[1]),
        name=name,
    )(jnp.reshape(scalar, (1,)).astype(jnp.int32), *args)


def fixed(shape):
    return pl.BlockSpec(shape, lambda g, sc: (0,) * len(shape))


def tile_of(width, most):
    return next(t for t in range(most, 0, -128) if width % t == 0)


def product(
    core, blocks, w, finish, outs, name, nt=False, extra=(), more=(), keep=False, send=False, at=None,
    most=1024,
):
    depth = blocks[0].shape[1]
    sizes = [at[0]] if at else [block.shape[0] for block in blocks]
    rows = sum(sizes)
    width = w.shape[0] if nt else w.shape[1]
    tile = tile_of(width, most)
    count = len(blocks)

    def kernel(sc, *refs):
        block_refs, w_ref = refs[:count], refs[count]
        extra_refs = refs[count + 1 : count + 1 + len(extra)]
        out_refs = refs[count + 1 + len(extra) :]
        step = pl.program_id(0)
        if keep:
            full_ref = out_refs[-1]

            @pl.when(step == 0)
            def _():
                start = 0
                for ref, size in zip(block_refs, sizes):
                    full_ref[start : start + size] = ref[...]
                    start += size
                if send:
                    side = pl.multiple_of((1 - sc[0]) * (depth // 2), 128)
                    out_refs[-2][:rows] = full_ref[:rows, pl.ds(side, depth // 2)]

            value = full_ref[:rows]
        else:
            value = block_refs[0][...]
        dot = dot_nt if nt else dot_nn
        finish(dot(value, w_ref[...]), extra_refs, out_refs, step, sc[0])

    w_spec = (
        pl.BlockSpec((tile, depth), lambda i, sc: (i, 0))
        if nt
        else pl.BlockSpec((depth, tile), lambda i, sc: (0, i))
    )
    tiled = lambda size: pl.BlockSpec((size, tile), lambda i, sc: (0, i))
    index = at[1] if at else 0
    return grid_call(
        kernel,
        core,
        (width // tile,),
        [pl.BlockSpec((size, depth), lambda i, sc: (index, 0)) for size in sizes]
        + [w_spec]
        + [tiled(array.shape[0]) for array in extra],
        [tiled(size) for size, _ in outs] + [fixed(shape) for shape in more],
        [jax.ShapeDtypeStruct((size, width), kind) for size, kind in outs]
        + [jax.ShapeDtypeStruct(shape, bf16) for shape in more],
        name,
        (*blocks, w, *extra),
        cost=(2 * rows * depth * width, 2 * (rows * depth + width * depth + rows * width)),
    )


def split_product(core, value, w, name, nt=False, parts=1, at=None):
    n = lax.axis_size("seq")
    size = (at[0] if at else value.shape[0]) // (n * parts)

    def finish(total, extra, outs, step, core):
        for p in range(parts):
            for k in range(n):
                start = (k * parts + p) * size
                ref = outs[p * n + k]
                ref[...] = total[start : start + size].astype(ref.dtype)

    outs = [(size, f32 if k == 0 else bf16) for p in range(parts) for k in range(n)]
    got = product(core, [value], w, finish, outs, name, nt=nt, at=at)
    return [list(got[p * n : (p + 1) * n]) for p in range(parts)]


def softmax_of(q, k, seg_col, seg_row):
    scores = dot_nt(q, k) * HEAD_DIM ** (-0.5)
    scores = jnp.where(seg_col == seg_row, scores, -1e30)
    terms = jnp.exp(scores - jnp.max(scores, axis=1, keepdims=True))
    return terms * (1.0 / jnp.sum(terms, axis=1, keepdims=True))


PAIR = 2


def head_of(ref, i):
    return ref[:, i * HEAD_DIM : (i + 1) * HEAD_DIM]


def attend_kernel(core, seg_col, seg_row, q, k, v, mixed):
    for i in range(PAIR):
        probs = softmax_of(head_of(q, i), head_of(k, i), seg_col[...], seg_row[...])
        result = dot_nn(probs.astype(bf16), head_of(v, i))
        mixed[:, i * HEAD_DIM : (i + 1) * HEAD_DIM] = result.astype(bf16)


def attend_back_kernel(core, seg_col, seg_row, q, k, v, gm, grad, sent):
    heads = pl.num_programs(0) * PAIR
    half = heads // 2
    scale = HEAD_DIM ** (-0.5)
    for i in range(PAIR):
        head = pl.program_id(0) * PAIR + i
        qi, ki, vi, gi = (head_of(ref, i) for ref in (q, k, v, gm))
        probs = softmax_of(qi, ki, seg_col[...], seg_row[...])
        grad_probs = dot_nt(gi, vi)
        products = jnp.sum(probs * grad_probs, axis=1, keepdims=True)
        grad_scores = (probs * (grad_probs - products)).astype(bf16)
        values = (
            dot_nn(grad_scores, ki) * scale,
            dot_tn(grad_scores, qi) * scale,
            dot_tn(probs.astype(bf16), gi),
        )
        for part, value in enumerate(values):
            start = pl.multiple_of((part * heads + head) * HEAD_DIM, HEAD_DIM)
            grad[:, pl.ds(start, HEAD_DIM)] = value.astype(bf16)

        @pl.when(head // half != core[0])
        def _():
            for part, value in enumerate(values):
                into = pl.multiple_of((part * half + head % half) * HEAD_DIM, HEAD_DIM)
                sent[:, pl.ds(into, HEAD_DIM)] = value.astype(bf16)


def head_spec(rows, offset):
    return pl.BlockSpec((rows, PAIR * HEAD_DIM), lambda h, sc: (0, offset // PAIR + h))


def qkv_specs(rows, heads):
    return [
        fixed((rows, 1)),
        fixed((1, rows)),
        head_spec(rows, 0),
        head_spec(rows, heads),
        head_spec(rows, 2 * heads),
    ]


def attend(qkv, seg, core):
    rows, width = qkv.shape
    heads = width // (3 * HEAD_DIM)
    return grid_call(
        attend_kernel,
        core,
        (heads // PAIR,),
        qkv_specs(rows, heads),
        head_spec(rows, 0),
        jax.ShapeDtypeStruct((rows, width // 3), bf16),
        "attend",
        (seg[:, None], seg[None, :], qkv, qkv, qkv),
    )


def attend_back(qkv, grad_mixed, seg, core):
    rows, width = qkv.shape
    heads = width // (3 * HEAD_DIM)
    return grid_call(
        attend_back_kernel,
        core,
        (heads // PAIR,),
        qkv_specs(rows, heads) + [head_spec(rows, 0)],
        [fixed((rows, width)), fixed((rows, width // 2))],
        [
            jax.ShapeDtypeStruct((rows, width), bf16),
            jax.ShapeDtypeStruct((rows, width // 2), bf16),
        ],
        "attend_back",
        (seg[:, None], seg[None, :], qkv, qkv, qkv, grad_mixed),
        cost=(400_000_000_000, 1),
    )


def pack_columns(shard, parts, core):
    n = lax.axis_size("seq")
    rows, width = shard.shape
    part = width // (parts * n)

    def kernel(sc, shard_ref, out):
        for j in range(n):
            for p in range(parts):
                start = (p * n + j) * part
                out[j, :, p * part : (p + 1) * part] = shard_ref[:, start : start + part]

    out = (n, rows, part * parts)
    return grid_call(
        kernel,
        core,
        (1,),
        [fixed(shard.shape)],
        fixed(out),
        jax.ShapeDtypeStruct(out, shard.dtype),
        "pack",
        (shard,),
    )


def join_columns(pieces, parts, halves, core):
    n, rows, width = pieces.shape
    piece = width // (parts * halves)

    def kernel(sc, pieces_ref, out):
        for h in range(halves):
            for j in range(n):
                for p in range(parts):
                    start = (p * n + j) * halves * piece
                    if halves > 1:
                        side = jnp.bitwise_xor(sc[0], h)
                        start = pl.multiple_of(start + side * piece, piece)
                    at = (h * parts + p) * piece
                    value = pieces_ref[j, :, at : at + piece].astype(f32)
                    out[:, pl.ds(start, piece)] = value

    out = (rows, n * width)
    return grid_call(
        kernel,
        core,
        (1,),
        [fixed(pieces.shape)],
        fixed(out),
        jax.ShapeDtypeStruct(out, f32),
        "join_columns",
        (pieces,),
    )


def exchange(pieces):
    return lax.all_to_all(pieces, "seq", 0, 0)


def gather_dp(shard):
    full = lax.all_gather(shard, DP, axis=shard.ndim - 2, tiled=True)
    return full.reshape(-1, full.shape[-1])


def sum_over(value, axes):
    return lax.psum_scatter(value, axes, scatter_dimension=value.ndim - 2, tiled=True)


def to_partner(value):
    return lax.ppermute(value, "core", [(0, 1), (1, 0)])


def feed_grads(core, pairs, pre, ffn, far):
    n = lax.axis_size("seq")
    chips = lax.axis_size("chip")
    tokens = pre[0].shape[0]
    height = pairs[0].shape[1]
    width = far[0].shape[1]
    rows = height // (n * chips)
    parts = len(pairs)

    def kernel(sc, *refs):
        act_refs = refs[n * parts : (n + 1) * parts]
        pre_refs = refs[(n + 1) * parts : (n + 2) * parts]
        ffn_refs = refs[(n + 2) * parts : (n + 3) * parts]
        out = refs[-1]
        for j in range(n):
            joined = zip(refs[j * parts : (j + 1) * parts], pre_refs)
            out[j] = sum(dot_tn(a[...], b[...]) for a, b in joined).astype(bf16)
        total = sum(dot_tn(a[...], b[...]) for a, b in zip(act_refs, ffn_refs))
        out[n:] = total.astype(bf16).reshape(n, rows, width)

    def rows_spec(j):
        return pl.BlockSpec((tokens, rows), lambda o, sc: (0, j * chips + o))

    own_half = [pl.BlockSpec((tokens, width), lambda o, sc: (0, sc[0]))] * len(pre)
    far_top = [pl.BlockSpec((tokens, width), lambda o, sc: (0, 0))] * len(far)
    far_low = [pl.BlockSpec((tokens, width), lambda o, sc: (1, 0))] * len(far)
    act_spec = pl.BlockSpec((tokens, n * rows), lambda o, sc: (1, o))
    return grid_call(
        kernel,
        core,
        (chips,),
        [rows_spec(j) for j in range(n) for _ in range(parts)]
        + [act_spec] * parts
        + own_half
        + far_low
        + own_half
        + far_top,
        pl.BlockSpec((2 * n, rows, width), lambda o, sc: (0, o, 0)),
        jax.ShapeDtypeStruct((2 * n, chips * rows, width), bf16),
        "feed_grads",
        (*[pair for _ in range(n) for pair in pairs], *pairs, *pre, *far, *ffn, *far),
    )


def attn_grad(core, tok, tok_far, mixed, mixed_far, grad_qkv, qkv_far, grad_attn, attn_far):
    n = lax.axis_size("seq")
    chips = lax.axis_size("chip")
    tokens = tok.shape[0]
    half = qkv_far.shape[1] // 3
    out_cols = attn_far.shape[1]
    cols = out_cols // n
    rows = mixed.shape[1] // chips * 2
    steps = chips // 2

    def kernel(sc, *refs):
        own_refs, far_refs = refs[:n], refs[n : 2 * n]
        mo, mf, qo, ko, vo, qkv_f, ao, af, out = refs[2 * n :]
        side = (dot_tn(mo[...], ao[...]) + dot_tn(mf[...], af[...])).astype(bf16)
        own = jnp.concatenate([qo[...], ko[...], vo[...]], axis=1)
        for j in range(n):
            total = dot_tn(own_refs[j][...], own) + dot_tn(far_refs[j][...], qkv_f[...])
            out[j, :, : 3 * half] = total.astype(bf16)
            out[j, :, 3 * half :] = side[:, j * cols : (j + 1) * cols]

    def rows_spec(j):
        return pl.BlockSpec((tokens, rows), lambda o, sc: (0, j * steps + o))

    def part_spec(p):
        return pl.BlockSpec((tokens, half), lambda o, sc: (0, 2 * p + sc[0]))

    width = 3 * half + cols
    return grid_call(
        kernel,
        core,
        (steps,),
        [rows_spec(j) for j in range(n)] * 2
        + [rows_spec(0)] * 2
        + [part_spec(p) for p in range(3)]
        + [
            fixed((tokens, 3 * half)),
            pl.BlockSpec((tokens, out_cols), lambda o, sc: (0, sc[0])),
            fixed((tokens, out_cols)),
        ],
        pl.BlockSpec((n, rows, width), lambda o, sc: (0, o, 0)),
        jax.ShapeDtypeStruct((n, steps * rows, width), bf16),
        "attn_grad",
        (
            *[tok] * n,
            *[tok_far] * n,
            mixed,
            mixed_far,
            *[grad_qkv] * 3,
            qkv_far,
            grad_attn,
            attn_far,
        ),
    )


def pick(value, axis, index):
    return lax.dynamic_index_in_dim(value, index, axis, keepdims=False)


def swap_rows(total, split, axis, core):
    value = total.reshape(split)
    return pick(value, axis, core), to_partner(pick(value, axis, 1 - core).astype(bf16))


def join_halves(own, far, core):
    return jnp.where(
        core == 0, jnp.concatenate([own, far], axis=-1), jnp.concatenate([far, own], axis=-1)
    )


def device_count():
    return lax.axis_size("seq") * lax.axis_size("chip") * lax.axis_size("core")


def all_small(vectors):
    count = device_count()
    packed = jnp.concatenate(vectors)
    table = lax.all_to_all(jnp.broadcast_to(packed[None], (count, packed.shape[0])), ALL, 0, 0)
    out = []
    start = 0
    for vector in vectors:
        size = vector.shape[0]
        out.append(table[:, start : start + size].reshape(-1).astype(f32))
        start += size
    return out


def scatter_small(vectors):
    count = device_count()
    packed = jnp.concatenate([v.reshape(count, -1) for v in vectors], axis=1)
    mine = jnp.sum(lax.all_to_all(packed, ALL, 0, 0), axis=0)
    out = []
    start = 0
    for vector in vectors:
        size = vector.shape[0] // count
        out.append(mine[start : start + size])
        start += size
    return out


def gelu_parts(v):
    c = 0.7978845608028654
    square = v * v
    share = 0.5 + 0.5 * jnp.tanh(v * (c + 0.044715 * c * square))
    value = v * share
    slope = share + value * (1.0 - share) * (2 * c + 6 * 0.044715 * c * square)
    return value, slope


def per_device(
    tokens,
    doc_lengths,
    qkv_weight,
    qv_bias,
    out_weight,
    out_bias,
    norm1_gain,
    norm1_bias,
    in_weight,
    in_bias,
    down_weight,
    down_bias,
    norm2_gain,
    norm2_bias,
    cotangent,
):
    n = lax.axis_size("seq")
    chips = lax.axis_size("chip")
    s = lax.axis_index("seq")
    c = lax.axis_index("core")
    rows = tokens.shape[1]
    width = tokens.shape[2]
    part = width // n
    half = width // 2
    paired = part // chips % 128 == 0 and in_weight.shape[1] == n * width
    tok_rows = tokens[0]

    tok_blocks = gather_blocks(tok_rows)
    out_w = gather_dp(out_weight)
    qkv_moved = exchange(pack_columns(qkv_weight, 3, c))
    vectors = [qv_bias, out_bias, norm1_gain, norm1_bias]
    vectors += [in_bias, down_bias, norm2_gain, norm2_bias]
    small = all_small(after(vectors, qkv_moved))
    qv_full, out_b, gain_one, shift_one, in_b, down_b, gain_two, shift_two = small
    qkv_w = gather_dp(after(qkv_moved, out_w))
    in_moved = exchange(after(pack_columns(in_weight, 1, c), tok_blocks))
    down_w = gather_dp(after(down_weight, qkv_moved))

    ends = jnp.cumsum(doc_lengths[0])
    steps = jnp.arange(n * rows, dtype=jnp.int32)
    places = jnp.remainder(s - steps // rows, n) * rows + steps % rows
    seg = jnp.sum((places[:, None] >= ends[None, :]).astype(jnp.int32), axis=1)

    q_bias = lax.dynamic_slice_in_dim(qv_full, s * part, part)
    v_bias = lax.dynamic_slice_in_dim(qv_full, width + s * part, part)
    qkv_b = jnp.concatenate([q_bias, jnp.zeros((part,), f32), v_bias])

    def finish_qkv(total, extra, outs, step, core):
        outs[0][...] = (total + extra[0][...]).astype(bf16)

    total_rows = n * rows
    qkv, tok_full = product(
        c,
        tok_blocks,
        qkv_w,
        finish_qkv,
        [(total_rows, bf16)],
        "qkv",
        extra=(qkv_b[None],),
        more=[(total_rows, width)],
        keep=True,
    )
    mixed = attend(qkv, seg, c)
    size = rows // 2
    halves = range(2)
    cut = [slice(h * size, (h + 1) * size) for h in halves]
    attn_split = split_product(c, mixed, out_w, "out", parts=2)
    attn_blocks = [send_blocks(blocks) for blocks in attn_split]
    in_w = gather_dp(after(in_moved, attn_blocks[0]))
    hidden = in_w.shape[1]
    in_bias_own = lax.dynamic_slice_in_dim(in_b, s * hidden, hidden)

    first, normed_one, recip_one, first_blocks = [], [], [], []
    for h in halves:
        if h:
            attn_blocks[h] = after(attn_blocks[h], first[0], down_w)
        attn = total_of(attn_blocks[h]) + out_b
        normed, recip = normalize(tok_rows[cut[h]].astype(f32) + attn)
        normed_one.append(normed)
        recip_one.append(recip)
        first.append(normed * gain_one + shift_one)
        first_blocks.append(gather_blocks(first[h].astype(bf16)))

    first_blocks[0] = after(first_blocks[0], first[1])

    def finish_in(total, extra, outs, step, core):
        value, slope = gelu_parts(total + extra[0][...])
        outs[0][...] = slope.astype(bf16)
        tile = value.shape[1]
        start = pl.multiple_of(step * tile, tile)
        outs[1][:, pl.ds(start, tile)] = value.astype(bf16)

    def finish_pair(total, extra, outs, step, core):
        value, slope = gelu_parts(total + extra[0][...])
        outs[0][...] = slope.astype(bf16)
        tile = value.shape[1]
        start = pl.multiple_of(step * tile, tile)
        outs[1][rows_half:, pl.ds(start, tile)] = value.astype(bf16)

    rows_half = n * size
    act_slope, pairs, ffn_blocks, ffn_split = [], [], [], []
    for h in halves:
        if h:
            first_blocks[h] = after(first_blocks[h], ffn_split[0])
        args = (c, first_blocks[h], in_w)
        outs = [(rows_half, bf16)]
        bias = (in_bias_own[None],)
        if paired:
            more = [(2 * rows_half, width)]
            slope, pair = product(
                *args, finish_pair, outs, "in", extra=bias, more=more, keep=True, most=512
            )
            ffn_split += split_product(c, pair, down_w, "down", at=(rows_half, 1))
        else:
            more = [(rows_half, hidden), (rows_half, width)]
            slope, *pair = product(*args, finish_in, outs, "in", extra=bias, more=more, keep=True)
            ffn_split += split_product(c, pair[0], down_w, "down")
        act_slope.append(slope)
        pairs.append(pair)
        ffn_blocks.append(send_blocks(ffn_split[h]))

    ffn_blocks[0] = after(ffn_blocks[0], ffn_split[1])
    result, normed_two, grad_h2, grad_ffn, grad_blocks = [], [], [], [], []
    grad_out = cotangent[0].astype(f32)
    for h in halves:
        if h:
            ffn_blocks[h] = after(ffn_blocks[h], grad_ffn[0])
        ffn = total_of(ffn_blocks[h]) + down_b
        normed, recip = normalize(first[h] + ffn)
        normed_two.append(normed)
        result.append((normed * gain_two + shift_two).astype(bf16))
        grad_h2.append(norm_back(grad_out[cut[h]], normed, recip, gain_two))
        grad_ffn.append(grad_h2[h].astype(bf16))
        grad_blocks.append(gather_blocks(grad_ffn[h]))
    result = jnp.concatenate(result, axis=0)
    shift_two_grad = jnp.sum(grad_out, axis=0)
    gain_two_grad = sum(jnp.sum(grad_out[cut[h]] * normed_two[h], axis=0) for h in halves)
    down_b_grad = sum(jnp.sum(grad_ffn[h].astype(f32), axis=0) for h in halves)

    grad_blocks[0] = after(grad_blocks[0], grad_ffn[1])
    if paired:
        pairs_far = [to_partner(v) for v in pairs]
        grad_blocks = [after(grad_blocks[0], pairs_far), grad_blocks[1]]

    def finish_pre(total, extra, outs, step, core):
        value = (total * extra[0][...].astype(f32)).astype(bf16)
        outs[0][...] = value
        if paired:
            tile = value.shape[1]
            steps = hidden // (2 * tile)

            @pl.when(step // steps != core)
            def _():
                start = pl.multiple_of(step % steps * tile, tile)
                outs[1][rows_half:, pl.ds(start, tile)] = value

    grad_ffn_full, grad_pre, grad_sent, back_split, back_blocks = [], [], [], [], []
    for h in halves:
        if h:
            grad_blocks[h] = after(grad_blocks[h], back_split[0])
        sent = [(2 * rows_half, half)] if paired else []
        got = product(
            c,
            grad_blocks[h],
            down_w,
            finish_pre,
            [(rows_half, bf16)],
            "pre_grad",
            nt=True,
            extra=(act_slope[h],),
            more=sent + [(rows_half, width)],
            keep=True,
            send=paired,
        )
        grad_pre.append(got[0])
        grad_sent.append(got[1])
        grad_ffn_full.append(got[-1])
        back_split += split_product(c, grad_pre[h], in_w, "back", nt=True)
        back_blocks.append(send_blocks(back_split[h]))
    in_b_grad = sum(jnp.sum(v.astype(f32), axis=0) for v in grad_pre)
    back_blocks[0] = after(back_blocks[0], back_split[1])
    if paired:
        tok_far, mixed_far = to_partner(tok_full), to_partner(mixed)
        grad_far = [to_partner(v) for v in grad_sent]
        feed = (pairs + pairs_far, grad_pre, grad_ffn_full, grad_far)
        feed_low = feed_grads(after(c, back_split[1]), *feed)
        back_blocks[1], feed_low = lax.optimization_barrier((back_blocks[1], feed_low))
        feed_sum = sum_over(feed_low, "chip")
    else:
        act, first_full = (jnp.concatenate([p[i] for p in pairs], axis=0) for i in range(2))
        grad_ffn_full, grad_pre = (jnp.concatenate(v, axis=0) for v in (grad_ffn_full, grad_pre))
        down_low = dot_tn(act, grad_ffn_full).astype(bf16)
        in_low = dot_tn(first_full, grad_pre).astype(bf16).reshape(n, part, -1)
        down_w_grad = sum_over(down_low, DP).astype(f32)
        in_w_grad = join_columns(exchange(sum_over(in_low, DP)), 1, 1, c)
    grad_first, grad_h1, grad_attn, attn_blocks = [], [], [], []
    for h in halves:
        if h:
            back_blocks[h] = after(back_blocks[h], grad_attn[0])
        grad_first.append(grad_h2[h] + total_of(back_blocks[h]))
        grad_h1.append(norm_back(grad_first[h], normed_one[h], recip_one[h], gain_one))
        grad_attn.append(grad_h1[h].astype(bf16))
        attn_blocks.append(gather_blocks(grad_attn[h]))
    shift_one_grad = sum(jnp.sum(grad_first[h], axis=0) for h in halves)
    gain_one_grad = sum(jnp.sum(grad_first[h] * normed_one[h], axis=0) for h in halves)
    out_b_grad = sum(jnp.sum(grad_attn[h].astype(f32), axis=0) for h in halves)
    grad_h1 = jnp.concatenate(grad_h1, axis=0)

    def finish_mixed(total, extra, outs, step, core):
        outs[0][...] = total.astype(bf16)

    blocks = [attn_blocks[h][k] for k in range(n) for h in halves]
    grad_mixed, attn_sent, grad_attn_full = product(
        c,
        blocks,
        out_w,
        finish_mixed,
        [(total_rows, bf16)],
        "mixed_grad",
        nt=True,
        more=[(total_rows, half), (total_rows, width)],
        keep=True,
        send=True,
    )
    grad_qkv, qkv_sent = attend_back(qkv, grad_mixed, seg, c)

    def small_sums(grad_qkv):
        sums = jnp.sum(grad_qkv.astype(f32), axis=0)
        qv_grad = jnp.zeros((2 * width,), f32)
        qv_grad = lax.dynamic_update_slice_in_dim(qv_grad, sums[:part], s * part, 0)
        qv_grad = lax.dynamic_update_slice_in_dim(qv_grad, sums[2 * part :], width + s * part, 0)
        in_b_all = jnp.zeros((n * hidden,), f32)
        in_b_all = lax.dynamic_update_slice_in_dim(in_b_all, in_b_grad, s * hidden, 0)
        return scatter_small(
            [
                qv_grad,
                out_b_grad,
                gain_one_grad,
                shift_one_grad,
                in_b_all,
                down_b_grad,
                gain_two_grad,
                shift_two_grad,
            ]
        )

    if paired:
        attn_far = to_partner(attn_sent)
        args = (tok_full, tok_far, mixed, mixed_far)
        qkv_far = to_partner(qkv_sent)
        attn_low = attn_grad(c, *args, grad_qkv, qkv_far, grad_attn_full, attn_far)
        attn_sum = sum_over(attn_low, "chip")
        last_split = split_product(c, after(grad_qkv, attn_low), qkv_w, "last", nt=True)[0]
        last_blocks = send_blocks(last_split)
        small_grads = small_sums(after(grad_qkv, last_blocks[1]))
        last_blocks[-1] = after(last_blocks[-1], small_grads)
        feed_sum = after(feed_sum, last_blocks)
        in_own, in_far = swap_rows(feed_sum[:n], (n, 2, -1, half), 1, c)
        in_pieces = exchange(jnp.concatenate([in_own, in_far], axis=2))
        in_w_grad = join_columns(in_pieces, 1, 2, c)
        down_own, down_far = swap_rows(feed_sum[n:], (2, -1, half), 0, c)
        down_w_grad = join_halves(down_own.astype(f32), down_far.astype(f32), c)
        attn_sum = after(attn_sum, in_far, down_own)
        attn_own, attn_far = swap_rows(attn_sum, (n, 2, -1, half), 1, c)
        split = 3 * part // 2
        pieces = jnp.concatenate([attn_own[:, :, :split], attn_far[:, :, :split]], 2)
        qkv_w_grad = join_columns(exchange(pieces), 3, 2, c)
        out_own, out_far = (
            jnp.concatenate([v[j, :, split:] for j in range(n)], axis=1).astype(f32)
            for v in (attn_own, attn_far)
        )
        out_w_grad = join_halves(out_own, out_far, c)
    else:
        last_split = split_product(c, grad_qkv, qkv_w, "last", nt=True)[0]
        last_blocks = send_blocks(last_split)
        small_grads = small_sums(after(grad_qkv, last_split))
        attn_low = after(dot_tn(tok_full, grad_qkv).astype(bf16), last_split)
        out_w_grad = sum_over(dot_tn(mixed, grad_attn_full).astype(bf16), DP).astype(f32)
        pieces = exchange(sum_over(attn_low.reshape(n, part, -1), DP))
        qkv_w_grad = join_columns(pieces, 3, 1, c)
    last_blocks = after(last_blocks, small_grads)
    input_grad = (grad_h1 + total_of(last_blocks)).astype(bf16)
    return (
        result[None],
        input_grad[None],
        qkv_w_grad,
        small_grads[0],
        out_w_grad,
        small_grads[1],
        small_grads[2],
        small_grads[3],
        in_w_grad,
        small_grads[4],
        down_w_grad,
        small_grads[5],
        small_grads[6],
        small_grads[7],
    )


def solution(mesh):
    devices = mesh.devices
    split = jax.sharding.Mesh(devices.reshape(devices.shape[0], -1, 2), ALL)
    rows = P(ALL, None)
    flat = P(ALL)
    tok = P(DP, "seq", None)
    ins = (tok, P(DP, None), rows, flat, rows, *[flat] * 3, rows, flat, rows, *[flat] * 3, tok)
    outs = (tok, tok, rows, flat, rows, *[flat] * 3, rows, flat, rows, *[flat] * 3)
    return jax.shard_map(per_device, mesh=split, in_specs=ins, out_specs=outs, check_vma=False)
```

```python
import jax
import jax.numpy as jnp
from jax import lax
from jax.experimental import pallas as pl
from jax.experimental.pallas import tpu as pltpu
from jax.sharding import PartitionSpec as P

HEAD_DIM = 128
eps_norm = 1e-06
f32 = jnp.float32
bf16 = jnp.bfloat16
DP = ("chip", "core")
ALL = ("seq", "chip", "core")


def after(value, *others):
    return lax.optimization_barrier((value, *others))[0]


def shift(value, step):
    n = lax.axis_size("seq")
    return lax.ppermute(value, "seq", [(i, (i + step) % n) for i in range(n)])


def gather_blocks(rows):
    n = lax.axis_size("seq")
    return [rows] + [shift(rows, k) for k in range(1, n)]


def send_blocks(blocks):
    return [blocks[0]] + [shift(blocks[k], -k) for k in range(1, len(blocks))]


def total_of(blocks):
    total = blocks[0]
    for block in blocks[1:]:
        total = total + block.astype(f32)
    return total


def normalize(hidden):
    center = hidden - jnp.mean(hidden, axis=-1, keepdims=True)
    spread = jnp.mean(center * center, axis=-1, keepdims=True)
    recip = lax.rsqrt(spread + eps_norm)
    return (center * recip, recip)


def norm_back(grad_out, normed, recip, gain):
    scaled = grad_out * gain
    return recip * (
        scaled
        - jnp.mean(scaled, axis=-1, keepdims=True)
        - normed * jnp.mean(scaled * normed, axis=-1, keepdims=True)
    )


def dot_nn(a, b):
    return lax.dot_general(a, b, (((1,), (0,)), ((), ())), preferred_element_type=f32)


def dot_nt(a, b):
    return lax.dot_general(a, b, (((1,), (1,)), ((), ())), preferred_element_type=f32)


def dot_tn(a, b):
    return lax.dot_general(a, b, (((0,), (0,)), ((), ())), preferred_element_type=f32)


def grid_call(kernel, scalar, grid, in_specs, out_specs, out_shape, name, args, cost=None):
    grid_spec = pltpu.PrefetchScalarGridSpec(
        num_scalar_prefetch=1, grid=grid, in_specs=in_specs, out_specs=out_specs
    )
    return pl.pallas_call(
        kernel,
        grid_spec=grid_spec,
        out_shape=out_shape,
        compiler_params=pltpu.CompilerParams(vmem_limit_bytes=56 << 20),
        cost_estimate=cost
        and pl.CostEstimate(flops=cost[0], transcendentals=0, bytes_accessed=cost[1]),
        name=name,
    )(jnp.reshape(scalar, (1,)).astype(jnp.int32), *args)


def fixed(shape):
    return pl.BlockSpec(shape, lambda g, sc: (0,) * len(shape))


def tile_of(width, most):
    return next(t for t in range(most, 0, -128) if width % t == 0)


def product(
    core, blocks, w, finish, outs, name, nt=False, extra=(), more=(), keep=False, send=False, at=None,
    most=1024,
):
    depth = blocks[0].shape[1]
    sizes = [at[0]] if at else [block.shape[0] for block in blocks]
    rows = sum(sizes)
    width = w.shape[0] if nt else w.shape[1]
    tile = tile_of(width, most)
    count = len(blocks)

    def kernel(sc, *refs):
        block_refs, w_ref = refs[:count], refs[count]
        extra_refs = refs[count + 1 : count + 1 + len(extra)]
        out_refs = refs[count + 1 + len(extra) :]
        step = pl.program_id(0)
        if keep:
            full_ref = out_refs[-1]

            @pl.when(step == 0)
            def _():
                start = 0
                for ref, size in zip(block_refs, sizes):
                    full_ref[start : start + size] = ref[...]
                    start += size
                if send:
                    side = pl.multiple_of((1 - sc[0]) * (depth // 2), 128)
                    out_refs[-2][:rows] = full_ref[:rows, pl.ds(side, depth // 2)]

            value = full_ref[:rows]
        else:
            value = block_refs[0][...]
        dot = dot_nt if nt else dot_nn
        finish(dot(value, w_ref[...]), extra_refs, out_refs, step, sc[0])

    w_spec = (
        pl.BlockSpec((tile, depth), lambda i, sc: (i, 0))
        if nt
        else pl.BlockSpec((depth, tile), lambda i, sc: (0, i))
    )
    tiled = lambda size: pl.BlockSpec((size, tile), lambda i, sc: (0, i))
    index = at[1] if at else 0
    return grid_call(
        kernel,
        core,
        (width // tile,),
        [pl.BlockSpec((size, depth), lambda i, sc: (index, 0)) for size in sizes]
        + [w_spec]
        + [tiled(array.shape[0]) for array in extra],
        [tiled(size) for size, _ in outs] + [fixed(shape) for shape in more],
        [jax.ShapeDtypeStruct((size, width), kind) for size, kind in outs]
        + [jax.ShapeDtypeStruct(shape, bf16) for shape in more],
        name,
        (*blocks, w, *extra),
        cost=(2 * rows * depth * width, 2 * (rows * depth + width * depth + rows * width)),
    )


def split_product(core, value, w, name, nt=False, parts=1, at=None):
    n = lax.axis_size("seq")
    size = (at[0] if at else value.shape[0]) // (n * parts)

    def finish(total, extra, outs, step, core):
        for p in range(parts):
            for k in range(n):
                start = (k * parts + p) * size
                ref = outs[p * n + k]
                ref[...] = total[start : start + size].astype(ref.dtype)

    outs = [(size, f32 if k == 0 else bf16) for p in range(parts) for k in range(n)]
    got = product(core, [value], w, finish, outs, name, nt=nt, at=at)
    return [list(got[p * n : (p + 1) * n]) for p in range(parts)]


def softmax_of(q, k, seg_col, seg_row):
    scores = dot_nt(q, k) * HEAD_DIM ** (-0.5)
    scores = jnp.where(seg_col == seg_row, scores, -1e30)
    terms = jnp.exp(scores - jnp.max(scores, axis=1, keepdims=True))
    return terms * (1.0 / jnp.sum(terms, axis=1, keepdims=True))


PAIR = 2


def head_of(ref, i):
    return ref[:, i * HEAD_DIM : (i + 1) * HEAD_DIM]


def attend_kernel(core, seg_col, seg_row, q, k, v, mixed):
    for i in range(PAIR):
        probs = softmax_of(head_of(q, i), head_of(k, i), seg_col[...], seg_row[...])
        result = dot_nn(probs.astype(bf16), head_of(v, i))
        mixed[:, i * HEAD_DIM : (i + 1) * HEAD_DIM] = result.astype(bf16)


def attend_back_kernel(core, seg_col, seg_row, q, k, v, gm, grad, sent):
    heads = pl.num_programs(0) * PAIR
    half = heads // 2
    scale = HEAD_DIM ** (-0.5)
    for i in range(PAIR):
        head = pl.program_id(0) * PAIR + i
        qi, ki, vi, gi = (head_of(ref, i) for ref in (q, k, v, gm))
        probs = softmax_of(qi, ki, seg_col[...], seg_row[...])
        grad_probs = dot_nt(gi, vi)
        products = jnp.sum(probs * grad_probs, axis=1, keepdims=True)
        grad_scores = (probs * (grad_probs - products)).astype(bf16)
        values = (
            dot_nn(grad_scores, ki) * scale,
            dot_tn(grad_scores, qi) * scale,
            dot_tn(probs.astype(bf16), gi),
        )
        for part, value in enumerate(values):
            start = pl.multiple_of((part * heads + head) * HEAD_DIM, HEAD_DIM)
            grad[:, pl.ds(start, HEAD_DIM)] = value.astype(bf16)

        @pl.when(head // half != core[0])
        def _():
            for part, value in enumerate(values):
                into = pl.multiple_of((part * half + head % half) * HEAD_DIM, HEAD_DIM)
                sent[:, pl.ds(into, HEAD_DIM)] = value.astype(bf16)


def head_spec(rows, offset):
    return pl.BlockSpec((rows, PAIR * HEAD_DIM), lambda h, sc: (0, offset // PAIR + h))


def qkv_specs(rows, heads):
    return [
        fixed((rows, 1)),
        fixed((1, rows)),
        head_spec(rows, 0),
        head_spec(rows, heads),
        head_spec(rows, 2 * heads),
    ]


def attend(qkv, seg, core):
    rows, width = qkv.shape
    heads = width // (3 * HEAD_DIM)
    return grid_call(
        attend_kernel,
        core,
        (heads // PAIR,),
        qkv_specs(rows, heads),
        head_spec(rows, 0),
        jax.ShapeDtypeStruct((rows, width // 3), bf16),
        "attend",
        (seg[:, None], seg[None, :], qkv, qkv, qkv),
    )


def attend_back(qkv, grad_mixed, seg, core):
    rows, width = qkv.shape
    heads = width // (3 * HEAD_DIM)
    return grid_call(
        attend_back_kernel,
        core,
        (heads // PAIR,),
        qkv_specs(rows, heads) + [head_spec(rows, 0)],
        [fixed((rows, width)), fixed((rows, width // 2))],
        [
            jax.ShapeDtypeStruct((rows, width), bf16),
            jax.ShapeDtypeStruct((rows, width // 2), bf16),
        ],
        "attend_back",
        (seg[:, None], seg[None, :], qkv, qkv, qkv, grad_mixed),
        cost=(400_000_000_000, 1),
    )


def pack_columns(shard, parts, core):
    n = lax.axis_size("seq")
    rows, width = shard.shape
    part = width // (parts * n)

    def kernel(sc, shard_ref, out):
        for j in range(n):
            for p in range(parts):
                start = (p * n + j) * part
                out[j, :, p * part : (p + 1) * part] = shard_ref[:, start : start + part]

    out = (n, rows, part * parts)
    return grid_call(
        kernel,
        core,
        (1,),
        [fixed(shard.shape)],
        fixed(out),
        jax.ShapeDtypeStruct(out, shard.dtype),
        "pack",
        (shard,),
    )


def join_columns(pieces, parts, halves, core):
    n, rows, width = pieces.shape
    piece = width // (parts * halves)

    def kernel(sc, pieces_ref, out):
        for h in range(halves):
            for j in range(n):
                for p in range(parts):
                    start = (p * n + j) * halves * piece
                    if halves > 1:
                        side = jnp.bitwise_xor(sc[0], h)
                        start = pl.multiple_of(start + side * piece, piece)
                    at = (h * parts + p) * piece
                    value = pieces_ref[j, :, at : at + piece].astype(f32)
                    out[:, pl.ds(start, piece)] = value

    out = (rows, n * width)
    return grid_call(
        kernel,
        core,
        (1,),
        [fixed(pieces.shape)],
        fixed(out),
        jax.ShapeDtypeStruct(out, f32),
        "join_columns",
        (pieces,),
    )


def exchange(pieces):
    return lax.all_to_all(pieces, "seq", 0, 0)


def gather_dp(shard):
    full = lax.all_gather(shard, DP, axis=shard.ndim - 2, tiled=True)
    return full.reshape(-1, full.shape[-1])


def sum_over(value, axes):
    return lax.psum_scatter(value, axes, scatter_dimension=value.ndim - 2, tiled=True)


def to_partner(value):
    return lax.ppermute(value, "core", [(0, 1), (1, 0)])


def feed_grads(core, pairs, pre, ffn, far):
    n = lax.axis_size("seq")
    chips = lax.axis_size("chip")
    tokens = pre[0].shape[0]
    height = pairs[0].shape[1]
    width = far[0].shape[1]
    rows = height // (n * chips)
    parts = len(pairs)

    def kernel(sc, *refs):
        act_refs = refs[n * parts : (n + 1) * parts]
        pre_refs = refs[(n + 1) * parts : (n + 2) * parts]
        ffn_refs = refs[(n + 2) * parts : (n + 3) * parts]
        out = refs[-1]
        for j in range(n):
            joined = zip(refs[j * parts : (j + 1) * parts], pre_refs)
            out[j] = sum(dot_tn(a[...], b[...]) for a, b in joined).astype(bf16)
        total = sum(dot_tn(a[...], b[...]) for a, b in zip(act_refs, ffn_refs))
        out[n:] = total.astype(bf16).reshape(n, rows, width)

    def rows_spec(j):
        return pl.BlockSpec((tokens, rows), lambda o, sc: (0, j * chips + o))

    own_half = [pl.BlockSpec((tokens, width), lambda o, sc: (0, sc[0]))] * len(pre)
    far_top = [pl.BlockSpec((tokens, width), lambda o, sc: (0, 0))] * len(far)
    far_low = [pl.BlockSpec((tokens, width), lambda o, sc: (1, 0))] * len(far)
    act_spec = pl.BlockSpec((tokens, n * rows), lambda o, sc: (1, o))
    return grid_call(
        kernel,
        core,
        (chips,),
        [rows_spec(j) for j in range(n) for _ in range(parts)]
        + [act_spec] * parts
        + own_half
        + far_low
        + own_half
        + far_top,
        pl.BlockSpec((2 * n, rows, width), lambda o, sc: (0, o, 0)),
        jax.ShapeDtypeStruct((2 * n, chips * rows, width), bf16),
        "feed_grads",
        (*[pair for _ in range(n) for pair in pairs], *pairs, *pre, *far, *ffn, *far),
    )


def attn_grad(core, tok, tok_far, mixed, mixed_far, grad_qkv, qkv_far, grad_attn, attn_far):
    n = lax.axis_size("seq")
    chips = lax.axis_size("chip")
    tokens = tok.shape[0]
    half = qkv_far.shape[1] // 3
    out_cols = attn_far.shape[1]
    cols = out_cols // n
    rows = mixed.shape[1] // chips * 2
    steps = chips // 2

    def kernel(sc, *refs):
        own_refs, far_refs = refs[:n], refs[n : 2 * n]
        mo, mf, qo, ko, vo, qkv_f, ao, af, out = refs[2 * n :]
        side = (dot_tn(mo[...], ao[...]) + dot_tn(mf[...], af[...])).astype(bf16)
        own = jnp.concatenate([qo[...], ko[...], vo[...]], axis=1)
        for j in range(n):
            total = dot_tn(own_refs[j][...], own) + dot_tn(far_refs[j][...], qkv_f[...])
            out[j, :, : 3 * half] = total.astype(bf16)
            out[j, :, 3 * half :] = side[:, j * cols : (j + 1) * cols]

    def rows_spec(j):
        return pl.BlockSpec((tokens, rows), lambda o, sc: (0, j * steps + o))

    def part_spec(p):
        return pl.BlockSpec((tokens, half), lambda o, sc: (0, 2 * p + sc[0]))

    width = 3 * half + cols
    return grid_call(
        kernel,
        core,
        (steps,),
        [rows_spec(j) for j in range(n)] * 2
        + [rows_spec(0)] * 2
        + [part_spec(p) for p in range(3)]
        + [
            fixed((tokens, 3 * half)),
            pl.BlockSpec((tokens, out_cols), lambda o, sc: (0, sc[0])),
            fixed((tokens, out_cols)),
        ],
        pl.BlockSpec((n, rows, width), lambda o, sc: (0, o, 0)),
        jax.ShapeDtypeStruct((n, steps * rows, width), bf16),
        "attn_grad",
        (
            *[tok] * n,
            *[tok_far] * n,
            mixed,
            mixed_far,
            *[grad_qkv] * 3,
            qkv_far,
            grad_attn,
            attn_far,
        ),
    )


def pick(value, axis, index):
    return lax.dynamic_index_in_dim(value, index, axis, keepdims=False)


def swap_rows(total, split, axis, core):
    value = total.reshape(split)
    return pick(value, axis, core), to_partner(pick(value, axis, 1 - core).astype(bf16))


def join_halves(own, far, core):
    return jnp.where(
        core == 0, jnp.concatenate([own, far], axis=-1), jnp.concatenate([far, own], axis=-1)
    )


def device_count():
    return lax.axis_size("seq") * lax.axis_size("chip") * lax.axis_size("core")


def all_small(vectors):
    count = device_count()
    packed = jnp.concatenate(vectors)
    table = lax.all_to_all(jnp.broadcast_to(packed[None], (count, packed.shape[0])), ALL, 0, 0)
    out = []
    start = 0
    for vector in vectors:
        size = vector.shape[0]
        out.append(table[:, start : start + size].reshape(-1).astype(f32))
        start += size
    return out


def scatter_small(vectors):
    count = device_count()
    packed = jnp.concatenate([v.reshape(count, -1) for v in vectors], axis=1)
    mine = jnp.sum(lax.all_to_all(packed, ALL, 0, 0), axis=0)
    out = []
    start = 0
    for vector in vectors:
        size = vector.shape[0] // count
        out.append(mine[start : start + size])
        start += size
    return out


def gelu_parts(v):
    c = 0.7978845608028654
    square = v * v
    share = 0.5 + 0.5 * jnp.tanh(v * (c + 0.044715 * c * square))
    value = v * share
    slope = share + value * (1.0 - share) * (2 * c + 6 * 0.044715 * c * square)
    return value, slope


def per_device(
    tokens,
    doc_lengths,
    qkv_weight,
    qv_bias,
    out_weight,
    out_bias,
    norm1_gain,
    norm1_bias,
    in_weight,
    in_bias,
    down_weight,
    down_bias,
    norm2_gain,
    norm2_bias,
    cotangent,
):
    n = lax.axis_size("seq")
    chips = lax.axis_size("chip")
    s = lax.axis_index("seq")
    c = lax.axis_index("core")
    rows = tokens.shape[1]
    width = tokens.shape[2]
    part = width // n
    half = width // 2
    paired = part // chips % 128 == 0 and in_weight.shape[1] == n * width
    tok_rows = tokens[0]

    tok_blocks = gather_blocks(tok_rows)
    out_w = gather_dp(out_weight)
    qkv_moved = exchange(pack_columns(qkv_weight, 3, c))
    vectors = [qv_bias, out_bias, norm1_gain, norm1_bias]
    vectors += [in_bias, down_bias, norm2_gain, norm2_bias]
    small = all_small(after(vectors, qkv_moved))
    qv_full, out_b, gain_one, shift_one, in_b, down_b, gain_two, shift_two = small
    qkv_w = gather_dp(after(qkv_moved, out_w))
    in_moved = exchange(after(pack_columns(in_weight, 1, c), tok_blocks))
    down_w = gather_dp(after(down_weight, qkv_moved))

    ends = jnp.cumsum(doc_lengths[0])
    steps = jnp.arange(n * rows, dtype=jnp.int32)
    places = jnp.remainder(s - steps // rows, n) * rows + steps % rows
    seg = jnp.sum((places[:, None] >= ends[None, :]).astype(jnp.int32), axis=1)

    q_bias = lax.dynamic_slice_in_dim(qv_full, s * part, part)
    v_bias = lax.dynamic_slice_in_dim(qv_full, width + s * part, part)
    qkv_b = jnp.concatenate([q_bias, jnp.zeros((part,), f32), v_bias])

    def finish_qkv(total, extra, outs, step, core):
        outs[0][...] = (total + extra[0][...]).astype(bf16)

    total_rows = n * rows
    qkv, tok_full = product(
        c,
        tok_blocks,
        qkv_w,
        finish_qkv,
        [(total_rows, bf16)],
        "qkv",
        extra=(qkv_b[None],),
        more=[(total_rows, width)],
        keep=True,
    )
    mixed = attend(qkv, seg, c)
    size = rows // 2
    halves = range(2)
    cut = [slice(h * size, (h + 1) * size) for h in halves]
    attn_split = split_product(c, mixed, out_w, "out", parts=2)
    attn_blocks = [send_blocks(blocks) for blocks in attn_split]
    in_w = gather_dp(after(in_moved, attn_blocks[0]))
    hidden = in_w.shape[1]
    in_bias_own = lax.dynamic_slice_in_dim(in_b, s * hidden, hidden)

    first, normed_one, recip_one, first_blocks = [], [], [], []
    for h in halves:
        if h:
            attn_blocks[h] = after(attn_blocks[h], first[0], down_w)
        attn = total_of(attn_blocks[h]) + out_b
        normed, recip = normalize(tok_rows[cut[h]].astype(f32) + attn)
        normed_one.append(normed)
        recip_one.append(recip)
        first.append(normed * gain_one + shift_one)
        first_blocks.append(gather_blocks(first[h].astype(bf16)))

    first_blocks[0] = after(first_blocks[0], first[1])

    def finish_in(total, extra, outs, step, core):
        value, slope = gelu_parts(total + extra[0][...])
        outs[0][...] = slope.astype(bf16)
        tile = value.shape[1]
        start = pl.multiple_of(step * tile, tile)
        outs[1][:, pl.ds(start, tile)] = value.astype(bf16)

    def finish_pair(total, extra, outs, step, core):
        value, slope = gelu_parts(total + extra[0][...])
        outs[0][...] = slope.astype(bf16)
        tile = value.shape[1]
        start = pl.multiple_of(step * tile, tile)
        outs[1][rows_half:, pl.ds(start, tile)] = value.astype(bf16)

    rows_half = n * size
    act_slope, pairs, ffn_blocks, ffn_split = [], [], [], []
    for h in halves:
        if h:
            first_blocks[h] = after(first_blocks[h], ffn_split[0])
        args = (c, first_blocks[h], in_w)
        outs = [(rows_half, bf16)]
        bias = (in_bias_own[None],)
        if paired:
            more = [(2 * rows_half, width)]
            slope, pair = product(
                *args, finish_pair, outs, "in", extra=bias, more=more, keep=True, most=512
            )
            ffn_split += split_product(c, pair, down_w, "down", at=(rows_half, 1))
        else:
            more = [(rows_half, hidden), (rows_half, width)]
            slope, *pair = product(*args, finish_in, outs, "in", extra=bias, more=more, keep=True)
            ffn_split += split_product(c, pair[0], down_w, "down")
        act_slope.append(slope)
        pairs.append(pair)
        ffn_blocks.append(send_blocks(ffn_split[h]))

    ffn_blocks[0] = after(ffn_blocks[0], ffn_split[1])
    result, normed_two, grad_h2, grad_ffn, grad_blocks = [], [], [], [], []
    grad_out = cotangent[0].astype(f32)
    for h in halves:
        if h:
            ffn_blocks[h] = after(ffn_blocks[h], grad_ffn[0])
        ffn = total_of(ffn_blocks[h]) + down_b
        normed, recip = normalize(first[h] + ffn)
        normed_two.append(normed)
        result.append((normed * gain_two + shift_two).astype(bf16))
        grad_h2.append(norm_back(grad_out[cut[h]], normed, recip, gain_two))
        grad_ffn.append(grad_h2[h].astype(bf16))
        grad_blocks.append(gather_blocks(grad_ffn[h]))
    result = jnp.concatenate(result, axis=0)
    shift_two_grad = jnp.sum(grad_out, axis=0)
    gain_two_grad = sum(jnp.sum(grad_out[cut[h]] * normed_two[h], axis=0) for h in halves)
    down_b_grad = sum(jnp.sum(grad_ffn[h].astype(f32), axis=0) for h in halves)

    grad_blocks[0] = after(grad_blocks[0], grad_ffn[1])
    if paired:
        pairs_far = [to_partner(v) for v in pairs]
        grad_blocks = [after(grad_blocks[0], pairs_far), grad_blocks[1]]

    def finish_pre(total, extra, outs, step, core):
        value = (total * extra[0][...].astype(f32)).astype(bf16)
        outs[0][...] = value
        if paired:
            tile = value.shape[1]
            steps = hidden // (2 * tile)

            @pl.when(step // steps != core)
            def _():
                start = pl.multiple_of(step % steps * tile, tile)
                outs[1][rows_half:, pl.ds(start, tile)] = value

    grad_ffn_full, grad_pre, grad_sent, back_split, back_blocks = [], [], [], [], []
    for h in halves:
        if h:
            grad_blocks[h] = after(grad_blocks[h], back_split[0])
        sent = [(2 * rows_half, half)] if paired else []
        got = product(
            c,
            grad_blocks[h],
            down_w,
            finish_pre,
            [(rows_half, bf16)],
            "pre_grad",
            nt=True,
            extra=(act_slope[h],),
            more=sent + [(rows_half, width)],
            keep=True,
            send=paired,
        )
        grad_pre.append(got[0])
        grad_sent.append(got[1])
        grad_ffn_full.append(got[-1])
        back_split += split_product(c, grad_pre[h], in_w, "back", nt=True)
        back_blocks.append(send_blocks(back_split[h]))
    in_b_grad = sum(jnp.sum(v.astype(f32), axis=0) for v in grad_pre)
    back_blocks[0] = after(back_blocks[0], back_split[1])
    if paired:
        tok_far, mixed_far = to_partner(tok_full), to_partner(mixed)
        grad_far = [to_partner(v) for v in grad_sent]
        feed = (pairs + pairs_far, grad_pre, grad_ffn_full, grad_far)
        feed_low = feed_grads(after(c, back_split[1]), *feed)
        back_blocks[1], feed_low = lax.optimization_barrier((back_blocks[1], feed_low))
        feed_sum = sum_over(feed_low, "chip")
    else:
        act, first_full = (jnp.concatenate([p[i] for p in pairs], axis=0) for i in range(2))
        grad_ffn_full, grad_pre = (jnp.concatenate(v, axis=0) for v in (grad_ffn_full, grad_pre))
        down_low = dot_tn(act, grad_ffn_full).astype(bf16)
        in_low = dot_tn(first_full, grad_pre).astype(bf16).reshape(n, part, -1)
        down_w_grad = sum_over(down_low, DP).astype(f32)
        in_w_grad = join_columns(exchange(sum_over(in_low, DP)), 1, 1, c)
    grad_first, grad_h1, grad_attn, attn_blocks = [], [], [], []
    for h in halves:
        if h:
            back_blocks[h] = after(back_blocks[h], grad_attn[0])
        grad_first.append(grad_h2[h] + total_of(back_blocks[h]))
        grad_h1.append(norm_back(grad_first[h], normed_one[h], recip_one[h], gain_one))
        grad_attn.append(grad_h1[h].astype(bf16))
        attn_blocks.append(gather_blocks(grad_attn[h]))
    shift_one_grad = sum(jnp.sum(grad_first[h], axis=0) for h in halves)
    gain_one_grad = sum(jnp.sum(grad_first[h] * normed_one[h], axis=0) for h in halves)
    out_b_grad = sum(jnp.sum(grad_attn[h].astype(f32), axis=0) for h in halves)
    grad_h1 = jnp.concatenate(grad_h1, axis=0)

    def finish_mixed(total, extra, outs, step, core):
        outs[0][...] = total.astype(bf16)

    blocks = [attn_blocks[h][k] for k in range(n) for h in halves]
    grad_mixed, attn_sent, grad_attn_full = product(
        c,
        blocks,
        out_w,
        finish_mixed,
        [(total_rows, bf16)],
        "mixed_grad",
        nt=True,
        more=[(total_rows, half), (total_rows, width)],
        keep=True,
        send=True,
    )
    grad_qkv, qkv_sent = attend_back(qkv, grad_mixed, seg, c)

    def small_sums(grad_qkv):
        sums = jnp.sum(grad_qkv.astype(f32), axis=0)
        qv_grad = jnp.zeros((2 * width,), f32)
        qv_grad = lax.dynamic_update_slice_in_dim(qv_grad, sums[:part], s * part, 0)
        qv_grad = lax.dynamic_update_slice_in_dim(qv_grad, sums[2 * part :], width + s * part, 0)
        in_b_all = jnp.zeros((n * hidden,), f32)
        in_b_all = lax.dynamic_update_slice_in_dim(in_b_all, in_b_grad, s * hidden, 0)
        return scatter_small(
            [
                qv_grad,
                out_b_grad,
                gain_one_grad,
                shift_one_grad,
                in_b_all,
                down_b_grad,
                gain_two_grad,
                shift_two_grad,
            ]
        )

    if paired:
        attn_far = to_partner(attn_sent)
        args = (tok_full, tok_far, mixed, mixed_far)
        qkv_far = to_partner(qkv_sent)
        last_split = split_product(c, grad_qkv, qkv_w, "last", nt=True)[0]
        last_blocks = send_blocks(last_split)
        attn_low = attn_grad(after(c, last_split), *args, grad_qkv, qkv_far, grad_attn_full, attn_far)
        last_blocks[1], attn_low = lax.optimization_barrier((last_blocks[1], attn_low))
        attn_sum = sum_over(attn_low, "chip")
        small_grads = small_sums(after(grad_qkv, last_blocks[1]))
        last_blocks[-1] = after(last_blocks[-1], small_grads)
        feed_sum = after(feed_sum, last_blocks)
        in_own, in_far = swap_rows(feed_sum[:n], (n, 2, -1, half), 1, c)
        in_pieces = exchange(jnp.concatenate([in_own, in_far], axis=2))
        in_w_grad = join_columns(in_pieces, 1, 2, c)
        down_own, down_far = swap_rows(feed_sum[n:], (2, -1, half), 0, c)
        down_w_grad = join_halves(down_own.astype(f32), down_far.astype(f32), c)
        input_grad = (grad_h1 + total_of(last_blocks)).astype(bf16)
        attn_sum = after(attn_sum, in_far, down_own, input_grad)
        attn_own, attn_far = swap_rows(attn_sum, (n, 2, -1, half), 1, c)
        split = 3 * part // 2
        pieces = jnp.concatenate([attn_own[:, :, :split], attn_far[:, :, :split]], 2)
        qkv_w_grad = join_columns(exchange(pieces), 3, 2, c)
        out_own, out_far = (
            jnp.concatenate([v[j, :, split:] for j in range(n)], axis=1).astype(f32)
            for v in (attn_own, attn_far)
        )
        out_w_grad = join_halves(out_own, out_far, c)
    else:
        last_split = split_product(c, grad_qkv, qkv_w, "last", nt=True)[0]
        last_blocks = send_blocks(last_split)
        small_grads = small_sums(after(grad_qkv, last_split))
        attn_low = after(dot_tn(tok_full, grad_qkv).astype(bf16), last_split)
        out_w_grad = sum_over(dot_tn(mixed, grad_attn_full).astype(bf16), DP).astype(f32)
        pieces = exchange(sum_over(attn_low.reshape(n, part, -1), DP))
        qkv_w_grad = join_columns(pieces, 3, 1, c)
        last_blocks = after(last_blocks, small_grads)
        input_grad = (grad_h1 + total_of(last_blocks)).astype(bf16)
    return (
        result[None],
        input_grad[None],
        qkv_w_grad,
        small_grads[0],
        out_w_grad,
        small_grads[1],
        small_grads[2],
        small_grads[3],
        in_w_grad,
        small_grads[4],
        down_w_grad,
        small_grads[5],
        small_grads[6],
        small_grads[7],
    )


def solution(mesh):
    devices = mesh.devices
    split = jax.sharding.Mesh(devices.reshape(devices.shape[0], -1, 2), ALL)
    rows = P(ALL, None)
    flat = P(ALL)
    tok = P(DP, "seq", None)
    ins = (tok, P(DP, None), rows, flat, rows, *[flat] * 3, rows, flat, rows, *[flat] * 3, tok)
    outs = (tok, tok, rows, flat, rows, *[flat] * 3, rows, flat, rows, *[flat] * 3)
    return jax.shard_map(per_device, mesh=split, in_specs=ins, out_specs=outs, check_vma=False)
```
